32 devices in a mesh: dp: 8 (over z, y), tensor: 4 (over x, core).
Axes of the slice: x: 2, y: 2, z: 4, core: 2. Of those that a mesh axis runs over, the one named last changes fastest.
Arguments:
- tokens: bfloat16 [8, 512, 768], P('dp'), as said below
- cotangent: bfloat16 [8, 512, 768], P('dp'), may hold values from -6 to 6
- lengths: int32 [8], P('dp'), may hold values from 128 to 512, as said below
- in_weight: float32 [7, 768, 768], P(None, 'dp', 'tensor'), as said below
- out_weight: float32 [5, 768, 768], P(None, 'tensor', 'dp'), may hold values from -0.4375 to 0.4375
- in_bias: float32 [6, 768], P(None, 'tensor'), may hold values from -3 to 3
- norm_vec: float32 [6, 768], replicated, may hold values from 0.1 to 1.9
- in_moments: float32 [2, 7, 768, 768], P(None, None, 'dp', 'tensor'), as said below
- out_moments: float32 [2, 5, 768, 768], P(None, None, 'tensor', 'dp'), as said below
- bias_moments: float32 [2, 6, 768], P(None, None, 'tensor'), as said below
- norm_moments: float32 [2, 6, 768], replicated, as said below
Outputs:
- output: bfloat16 [8, 512, 768], P('dp')
- grad_input: bfloat16 [8, 512, 768], P('dp')
- in_grad: float32 [7, 768, 768], P(None, 'dp', 'tensor')
- out_grad: float32 [5, 768, 768], P(None, 'tensor', 'dp')
- bias_grad: float32 [6, 768], P(None, 'tensor')
- norm_grad: float32 [6, 768], replicated
- new_in_weight: float32 [7, 768, 768], P(None, 'dp', 'tensor')
- new_out_weight: float32 [5, 768, 768], P(None, 'tensor', 'dp')
- new_in_bias: float32 [6, 768], P(None, 'tensor')
- new_norm_vec: float32 [6, 768], replicated
- new_in_moments: float32 [2, 7, 768, 768], P(None, None, 'dp', 'tensor')
- new_out_moments: float32 [2, 5, 768, 768], P(None, None, 'tensor', 'dp')
- new_bias_moments: float32 [2, 6, 768], P(None, None, 'tensor')
- new_norm_moments: float32 [2, 6, 768], replicated
The draws below stay inside these ranges and needn't reach their ends.
Inputs may be any that keep to these rules, and one draw needn't show every extreme that they name: `lengths`: each sequence's live tokens come first; the first sequence is full, with 512 live tokens. `tokens`: entries lie within -6 and 6. `in_weight`: entries lie within -6 / sqrt(768) and 6 / sqrt(768). `in_moments`: second moments (index 1) are positive. `out_moments`: second moments (index 1) are positive. `bias_moments`: second moments (index 1) are positive. `norm_moments`: second moments (index 1) are positive.
All inputs are finite; a program needn't handle non-finite values.
Results may differ from the reference program's by a relative error of at most 0.023.
Values may be sent and summed in bfloat16 or wider, within the bound.
A program may use at most 128 MiB of HBM per device.

```python
import math
import jax
import jax.numpy as jnp
from jax import lax

D = 768
HEADS = 12
HDIM = 64
SEQ_LEN = 512
SEQ_DEV = 1
SEQS = 8
N_TENSOR = 4


token_bound = 6.0


def draw_tokens(key, part):
    base = jnp.clip(jax.random.normal(jax.random.fold_in(key, 31), (SEQS, SEQ_LEN, D), jnp.float32), -token_bound, token_bound)
    return base.astype(jnp.bfloat16)


def draw_in_weight(key, part):
    base = jnp.clip(jax.random.normal(jax.random.fold_in(key, 32), (7, D, D), jnp.float32), -token_bound, token_bound) * D ** (-0.5)
    return base


def draw_lengths(key, part):
    devices = SEQS // SEQ_DEV
    key_base = jax.random.fold_in(key, 11)
    key_factor = jax.random.fold_in(key, 12)
    lowest = max(1, SEQ_LEN // 4)
    base = jax.random.randint(key_base, (devices, SEQ_DEV), lowest, SEQ_LEN // 2 + 1)
    factor = jax.random.randint(key_factor, (devices, 1), 1, 3)
    sizes = jnp.minimum(base * factor, SEQ_LEN).reshape(SEQS)
    return sizes.at[0].set(SEQ_LEN).astype(jnp.int32)


def moment_pair(key, shape, salt):
    own_key = jax.random.fold_in(key, salt)
    key_first = jax.random.fold_in(own_key, 21)
    key_second = jax.random.fold_in(own_key, 22)
    first = 5.0 * jax.random.normal(key_first, shape, jnp.float32)
    second = jnp.exp(jax.random.uniform(key_second, shape, jnp.float32, math.log(0.5), math.log(20.0)))
    return jnp.stack([first, second])


def draw_in_moments(key, part):
    return moment_pair(key, (7, D, D), 101)


def draw_out_moments(key, part):
    return moment_pair(key, (5, D, D), 102)


def draw_bias_moments(key, part):
    return moment_pair(key, (6, D), 103)


def draw_norm_moments(key, part):
    return moment_pair(key, (6, D), 104)


def block_scale(key, dims, pieces, least, high):
    loudness = 1.0
    for axis_at, parts in pieces:
        heights = jax.random.uniform(jax.random.fold_in(jax.random.fold_in(key, 6), axis_at), (parts,), jnp.float32, least / len(pieces), high / len(pieces))
        loudness = loudness * jnp.repeat(jnp.exp(heights), dims[axis_at] // parts).reshape((-1,) + (1,) * (len(dims) - 1 - axis_at))
    return loudness


def scatter_about(key, shape, width, most, shards=(), kind=jnp.bfloat16):
    result = jax.random.normal(key, shape, jnp.float32) * width
    if len(shards) > 0:
        result = block_scale(key, shape, shards, -0.22, 0.18) * result
    return jnp.clip(result, min=-most, max=most).astype(kind)


def setup_inputs(seed: int = 0) -> dict:
    streams_of = jax.random.split(jax.random.key(seed), 12)
    tokens = draw_tokens(jax.random.fold_in(streams_of[11], 71), 0)
    cotangent = scatter_about(streams_of[1], (SEQS, SEQ_LEN, D), 1.0, 6.0, ((0, 8),))
    lengths = draw_lengths(jax.random.fold_in(streams_of[11], 71), 0)
    in_weight = draw_in_weight(jax.random.fold_in(streams_of[11], 71), 0)
    out_weight = scatter_about(streams_of[4], (5, D, D), (D // 4) ** -0.5, 0.4375, ((1, 4), (2, 8)), jnp.float32)
    in_bias = scatter_about(streams_of[5], (6, D), 0.5, 3.0, ((1, 4),), jnp.float32)
    norm_vec = jnp.clip(1.0 + 0.18 * jax.random.normal(streams_of[6], (6, D), jnp.float32), 0.1, 1.9)
    in_moments = draw_in_moments(jax.random.fold_in(streams_of[11], 71), 0)
    out_moments = draw_out_moments(jax.random.fold_in(streams_of[11], 71), 0)
    bias_moments = draw_bias_moments(jax.random.fold_in(streams_of[11], 71), 0)
    norm_moments = draw_norm_moments(jax.random.fold_in(streams_of[11], 71), 0)
    return {"tokens": tokens, "cotangent": cotangent, "lengths": lengths, "in_weight": in_weight, "out_weight": out_weight, "in_bias": in_bias, "norm_vec": norm_vec, "in_moments": in_moments, "out_moments": out_moments, "bias_moments": bias_moments, "norm_moments": norm_moments}


norm_eps = 1e-12
masked_score = -1e+30
learn_rate = 0.005
beta_first = 0.9
beta_second = 0.999
adam_eps = 1e-08
weight_decay = 0.01
step_count = 2.0
root_half = 0.7071067811865476
normal_peak = 0.3989422804014327

def matmul(left_op, right_op):
    return jnp.dot(left_op, right_op, preferred_element_type=jnp.float32)

def rounded_wide(values):
    return lax.optimization_barrier(values.astype(jnp.bfloat16)).astype(jnp.float32)

def layer_norm(summed_rows, gain_vec, shift_vec):
    center = lax.optimization_barrier(jnp.mean(summed_rows, -1, keepdims=True))
    offset = summed_rows - center
    inverse = lax.rsqrt(lax.optimization_barrier(jnp.mean(offset * offset, -1, keepdims=True)) + norm_eps)
    normed = offset * inverse
    return (normed * gain_vec + shift_vec, normed, inverse)

def norm_back(upstream, normed, inverse, gain_vec):
    scaled = upstream * gain_vec
    return inverse * (scaled - lax.optimization_barrier(jnp.mean(scaled, -1, keepdims=True)) - normed * lax.optimization_barrier(jnp.mean(scaled * normed, -1, keepdims=True)))

def gelu_value(pre_act):
    return 0.5 * pre_act * (1.0 + jax.scipy.special.erf(pre_act * root_half))

def gelu_slope(pre_act):
    return 0.5 * (1.0 + jax.scipy.special.erf(pre_act * root_half)) + pre_act * jnp.exp(-0.5 * pre_act * pre_act) * normal_peak

def tensor_sum(partials):
    return lax.optimization_barrier(jnp.sum(rounded_wide(partials), 0))

def adam_update(param, grad, moments, decay):
    first = beta_first * moments[0] + (1.0 - beta_first) * grad
    second = beta_second * moments[1] + (1.0 - beta_second) * grad * grad
    first_hat = first / (1.0 - beta_first ** step_count)
    second_hat = second / (1.0 - beta_second ** step_count)
    new_param = param - learn_rate * (first_hat / (jnp.sqrt(second_hat) + adam_eps) + decay * param)
    return (new_param, jnp.stack([first, second]))

def reference(tokens, cotangent, lengths, in_weight, out_weight, in_bias, norm_vec, in_moments, out_moments, bias_moments, norm_moments):
    group_width = D // N_TENSOR
    in_low = in_weight.astype(jnp.bfloat16)
    out_low = out_weight.astype(jnp.bfloat16)
    w_query, w_key, w_value = (in_low[0], in_low[1], in_low[2])
    w_proj = out_low[0]
    up_wide = in_low[3:7].astype(jnp.float32)
    down_wide = out_low[1:5].astype(jnp.float32)
    up_groups = up_wide.reshape(4, D, N_TENSOR, group_width)
    down_groups = down_wide.reshape(4, N_TENSOR, group_width, D)
    proj_groups = w_proj.astype(jnp.float32).reshape(N_TENSOR, group_width, D)
    query_groups = w_query.astype(jnp.float32).reshape(D, N_TENSOR, group_width)
    key_groups = w_key.astype(jnp.float32).reshape(D, N_TENSOR, group_width)
    value_groups = w_value.astype(jnp.float32).reshape(D, N_TENSOR, group_width)
    scale_factor = HDIM ** (-0.5)

    def one_sequence(carry, operands):
        seq_tokens, seq_cot, length = operands
        positions = lax.broadcasted_iota(jnp.int32, (SEQ_LEN,), 0)
        usable = positions < length
        live_rows = usable.astype(jnp.float32)
        query = (matmul(seq_tokens, w_query) + in_bias[0]).astype(jnp.bfloat16)
        keys_low = matmul(seq_tokens, w_key).astype(jnp.bfloat16)
        values_low = (matmul(seq_tokens, w_value) + in_bias[1]).astype(jnp.bfloat16)
        query_heads = query.astype(jnp.float32).reshape(SEQ_LEN, HEADS, HDIM)
        key_heads = keys_low.astype(jnp.float32).reshape(SEQ_LEN, HEADS, HDIM)
        value_heads = values_low.astype(jnp.float32).reshape(SEQ_LEN, HEADS, HDIM)
        scores = jnp.einsum('qhe,khe->hqk', query_heads, key_heads) * scale_factor
        scores = jnp.where(usable[None, None, :], scores, masked_score)
        highest = lax.optimization_barrier(jnp.max(scores, -1, keepdims=True))
        log_total = highest + jnp.log(lax.optimization_barrier(jnp.sum(jnp.exp(scores - highest), -1, keepdims=True)))
        probs = jnp.exp(scores - log_total)
        probs_low = rounded_wide(probs)
        mixed = jnp.einsum('hqk,khe->qhe', probs_low, value_heads).reshape(SEQ_LEN, D).astype(jnp.bfloat16)
        mixed_wide = mixed.astype(jnp.float32)
        attn = tensor_sum(jnp.einsum('ltc,tcd->tld', mixed_wide.reshape(SEQ_LEN, N_TENSOR, group_width), proj_groups))
        hidden, normed_one, inverse_one = layer_norm(seq_tokens.astype(jnp.float32) + attn + norm_vec[0], norm_vec[1], norm_vec[2])
        hidden_low = hidden.astype(jnp.bfloat16)
        hidden_wide = hidden_low.astype(jnp.float32)
        pre_act = jnp.einsum('ld,kdc->lkc', hidden_wide, up_wide) + in_bias[2:6]
        act_low = gelu_value(pre_act).astype(jnp.bfloat16)
        act_wide = act_low.astype(jnp.float32)
        ffn = tensor_sum(jnp.einsum('lktj,ktjd->tld', act_wide.reshape(SEQ_LEN, 4, N_TENSOR, group_width), down_groups))
        out_rows, normed_two, inverse_two = layer_norm(hidden + ffn + norm_vec[3], norm_vec[4], norm_vec[5])
        grad_out = seq_cot.astype(jnp.float32) * live_rows[:, None]
        grad_two = norm_back(grad_out, normed_two, inverse_two, norm_vec[4])
        grad_two_low = grad_two.astype(jnp.bfloat16)
        grad_two_wide = grad_two_low.astype(jnp.float32)
        grad_act = jnp.einsum('ld,kcd->lkc', grad_two_wide, down_wide)
        grad_pre = grad_act * gelu_slope(pre_act)
        grad_pre_low = grad_pre.astype(jnp.bfloat16)
        grad_pre_wide = grad_pre_low.astype(jnp.float32)
        grad_hidden = grad_two + tensor_sum(jnp.einsum('lktj,kdtj->tld', grad_pre_wide.reshape(SEQ_LEN, 4, N_TENSOR, group_width), up_groups))
        grad_one = norm_back(grad_hidden, normed_one, inverse_one, norm_vec[1])
        grad_one_low = grad_one.astype(jnp.bfloat16)
        grad_mixed = jnp.dot(grad_one_low, w_proj.T, preferred_element_type=jnp.float32).astype(jnp.bfloat16)
        grad_heads = grad_mixed.astype(jnp.float32).reshape(SEQ_LEN, HEADS, HDIM)
        grad_probs = jnp.einsum('qhe,khe->hqk', grad_heads, value_heads)
        row_dot = lax.optimization_barrier(jnp.sum(probs * grad_probs, -1, keepdims=True))
        grad_scores = rounded_wide(probs * (grad_probs - row_dot) * scale_factor)
        grad_query = jnp.einsum('hqk,khe->qhe', grad_scores, key_heads).reshape(SEQ_LEN, D)
        grad_keys = jnp.einsum('hqk,qhe->khe', grad_scores, query_heads).reshape(SEQ_LEN, D)
        grad_values = jnp.einsum('hqk,qhe->khe', probs_low, grad_heads).reshape(SEQ_LEN, D)
        query_low = grad_query.astype(jnp.bfloat16)
        keys_grad_low = grad_keys.astype(jnp.bfloat16)
        values_grad_low = grad_values.astype(jnp.bfloat16)
        input_parts = jnp.einsum('ltj,dtj->tld', query_low.astype(jnp.float32).reshape(SEQ_LEN, N_TENSOR, group_width), query_groups)
        input_parts = input_parts + jnp.einsum('ltj,dtj->tld', keys_grad_low.astype(jnp.float32).reshape(SEQ_LEN, N_TENSOR, group_width), key_groups)
        input_parts = input_parts + jnp.einsum('ltj,dtj->tld', values_grad_low.astype(jnp.float32).reshape(SEQ_LEN, N_TENSOR, group_width), value_groups)
        grad_input = (grad_one + tensor_sum(input_parts)).astype(jnp.bfloat16)
        grad_up = jnp.einsum('ld,lkc->kdc', hidden_wide, grad_pre_wide)
        grad_in = jnp.concatenate([jnp.stack([matmul(seq_tokens.T, query_low), matmul(seq_tokens.T, keys_grad_low), matmul(seq_tokens.T, values_grad_low)]), grad_up], 0)
        grad_down = jnp.einsum('lkc,ld->kcd', act_wide, grad_two_wide)
        grad_outw = jnp.concatenate([matmul(mixed.T, grad_one_low)[None], grad_down], 0)
        grad_bias = jnp.concatenate([jnp.stack([lax.optimization_barrier(jnp.sum(grad_query, 0)), lax.optimization_barrier(jnp.sum(grad_values, 0))]), lax.optimization_barrier(jnp.sum(grad_pre, 0))], 0)
        grad_norm = jnp.stack([lax.optimization_barrier(jnp.sum(grad_one, 0)), lax.optimization_barrier(jnp.sum(grad_hidden * normed_one, 0)), lax.optimization_barrier(jnp.sum(grad_hidden, 0)), lax.optimization_barrier(jnp.sum(grad_two, 0)), lax.optimization_barrier(jnp.sum(grad_out * normed_two, 0)), lax.optimization_barrier(jnp.sum(grad_out, 0))])
        new_carry = (carry[0] + grad_in, carry[1] + grad_outw, carry[2] + grad_bias, carry[3] + grad_norm)
        return (new_carry, (out_rows.astype(jnp.bfloat16), grad_input))
    start = (jnp.zeros((7, D, D), jnp.float32), jnp.zeros((5, D, D), jnp.float32), jnp.zeros((6, D), jnp.float32), jnp.zeros((6, D), jnp.float32))
    totals, outputs = lax.scan(one_sequence, start, (tokens, cotangent, lengths))
    in_grad, out_grad, bias_grad, norm_grad = totals
    new_in_weight, new_in_moments = adam_update(in_weight, in_grad, in_moments, weight_decay)
    new_out_weight, new_out_moments = adam_update(out_weight, out_grad, out_moments, weight_decay)
    new_in_bias, new_bias_moments = adam_update(in_bias, bias_grad, bias_moments, 0.0)
    new_norm_vec, new_norm_moments = adam_update(norm_vec, norm_grad, norm_moments, 0.0)
    return (outputs[0], outputs[1], in_grad, out_grad, bias_grad, norm_grad, new_in_weight, new_out_weight, new_in_bias, new_norm_vec, new_in_moments, new_out_moments, new_bias_moments, new_norm_moments)
```

```python
import functools

import jax
import jax.numpy as jnp
from jax import lax
from jax.experimental import pallas as pl
from jax.experimental.pallas import tpu as pltpu
from jax.sharding import PartitionSpec as P

HDIM = 64


norm_eps = 1e-12
masked_score = -1e30
learn_rate = 0.005
beta_first = 0.9
beta_second = 0.999
adam_eps = 1e-08
weight_decay = 0.01
step_count = 2.0
root_half = 0.7071067811865476
normal_peak = 0.3989422804014327


RING = 8
CHUNKS = 4
HEADS_HERE = 3
MESH = pl.DeviceIdType.MESH
ATTN, UP, DOWN = 0, 1, 2
SUM_ATTN, SUM_FFN, SUM_BACK, SUM_INPUT = 0, 1, 2, 3
EX_HIDDEN, EX_OUT, EX_TWO, EX_ONE, EX_INPUT = 0, 1, 2, 3, 4


def ring_place(index):
    depth, side = index // 2, index % 2
    return depth + side * (RING - 1 - 2 * depth)


def ring_device(place):
    side = place // (RING // 2)
    depth = place + side * (RING - 1 - 2 * place)
    return 2 * depth + side


def dot_nn(left_op, right_op):
    return jnp.dot(left_op, right_op, preferred_element_type=jnp.float32)


def dot_nt(left_op, right_op):
    return lax.dot_general(
        left_op, right_op, (((1,), (1,)), ((), ())), preferred_element_type=jnp.float32
    )


def normalize(rows):
    center = jnp.mean(rows, -1, keepdims=True)
    offset = rows - center
    inverse = lax.rsqrt(jnp.mean(offset * offset, -1, keepdims=True) + norm_eps)
    return offset * inverse, inverse


def column_sum(rows):
    return jnp.sum(rows, 0, keepdims=True)


INPUTS = ("tokens_hbm", "cot_hbm", "lengths", "inw_hbm", "outw_hbm", "bias_hbm", "norm_hbm")
OUTPUTS = ("out", "gin", "tot0", "tot1", "tot2", "norm_out", "bias_out")


def scratch_list(rows, width, slab, group):
    own = rows // (2 * CHUNKS)
    piece = slab // 2
    low, wide = jnp.bfloat16, jnp.float32
    dma = pltpu.SemaphoreType.DMA
    vmem = pltpu.VMEM
    heads = (HEADS_HERE, rows, HDIM)
    turned = (HEADS_HERE, HDIM, rows)
    return {
        "tokens": vmem((rows, width), low),
        "cot": vmem((rows, width), low),
        "inw": vmem((7, slab, group), wide),
        "outw": vmem((5, group, slab), wide),
        "bias": vmem((6, group), wide),
        "norm": vmem((6, width), wide),
        "full": vmem((3, width, width), low),
        "grads": vmem((3, width, width), low),
        "arrived": vmem((3, 4, 2, 2, piece, width), low),
        "leaving": vmem((3, 4, 2, 2, piece, width), low),
        "tokens_t": vmem((width, rows), low),
        "qkv_bias": vmem((1, width), wide),
        "up_bias": vmem((1, width), wide),
        "query": vmem(heads, low),
        "key": vmem(heads, low),
        "value": vmem(heads, low),
        "dmix": vmem(heads, low),
        "key_t": vmem(turned, low),
        "value_t": vmem(turned, low),
        "probs": vmem((HEADS_HERE, rows, rows), wide),
        "mixed_t": vmem((group, rows), low),
        "mixed": vmem((rows, group), low),
        "dquery_t": vmem((group, rows), wide),
        "dqkv": vmem((rows, width), low),
        "part": vmem((4, rows, width), low),
        "near": vmem((4, CHUNKS, own, width), low),
        "chip": vmem((4, CHUNKS, own, width), low),
        "far": vmem((4, CHUNKS, own, width), low),
        "hidden": vmem((CHUNKS, own, width), wide),
        "normed1": vmem((CHUNKS, own, width), wide),
        "inverse1": vmem((CHUNKS, own, 1), wide),
        "dres2": vmem((CHUNKS, own, width), wide),
        "dres1": vmem((CHUNKS, own, width), wide),
        "hidden_low": vmem((rows, width), low),
        "dres2_low": vmem((rows, width), low),
        "dres1_low": vmem((rows, width), low),
        "act": vmem((rows, width), low),
        "slope": vmem((rows, width), wide),
        "dpre_low": vmem((rows, width), low),
        "norm_acc": vmem((CHUNKS, 8, width), wide),
        "bias_acc": vmem((CHUNKS, 1, width), wide),
        "norm_half": vmem((2, 8, width // 2), wide),
        "norm_in": vmem((8, width // 2), wide),
        "small": vmem((8, 640), wide),
        "norm_fin": vmem((2, 8, width // 2), wide),
        "turned": vmem((width, rows), low),
        "slots": vmem((RING, 8, 640), wide),
        "load_sem": dma((6,)),
        "g_send": dma((3, 4, 2, 2)),
        "g_recv": dma((3, 4, 2, 2)),
        "s_send": dma((3, 4, 2, 2)),
        "s_recv": dma((3, 4, 2, 2)),
        "near_send": dma((4, CHUNKS)),
        "near_recv": dma((4, CHUNKS)),
        "far_send": dma((4, CHUNKS)),
        "far_recv": dma((4, CHUNKS)),
        "ex_send": dma((5, CHUNKS)),
        "ex_recv": dma((5, CHUNKS)),
        "dp_send": dma((RING - 1,)),
        "dp_recv": dma((RING - 1,)),
        "pair_send": dma((2,)),
        "pair_recv": dma((2,)),
    }


class Names:
    pass


def layer_kernel(names, *refs):
    k = Names()
    for name, ref in zip(names, refs):
        setattr(k, name, ref)
    rows, width = k.tokens.shape
    group, slab = k.bias.shape[1], k.inw.shape[1]
    span = rows // CHUNKS
    own = span // 2
    piece = slab // 2
    low, wide = jnp.bfloat16, jnp.float32
    me, tensor = lax.axis_index("dp"), lax.axis_index("tensor")
    core = tensor % 2
    partner, across = tensor + 1 - 2 * core, (tensor + 2) % 4
    place = ring_place(me)
    targets = (ring_device((place + 1) % RING), ring_device((place + RING - 1) % RING))
    sent = []

    def send(source, target, send_sem, recv_sem, device):
        copy = pltpu.make_async_remote_copy(
            src_ref=source,
            dst_ref=target,
            send_sem=send_sem,
            recv_sem=recv_sem,
            device_id=device,
            device_id_type=MESH,
        )
        copy.start()
        sent.append(copy)
        return copy

    def slab_rows(owner, half):
        return pl.ds(pl.multiple_of(owner * slab + half * piece, piece), piece)

    def gather_steps(index):
        copies = {}
        for step in range(4):
            for half in range(2):
                for way in range(2):
                    if step == 3 and half != way:
                        continue
                    shift = RING - step if way == 0 else step
                    spot = k.full.at[index, slab_rows(ring_device((place + shift) % RING), half)]
                    if step:
                        copies[step - 1, half, way].wait_recv()
                    spots = (index, step, half, way)
                    copies[step, half, way] = send(
                        spot, spot, k.g_send.at[spots], k.g_recv.at[spots], {"dp": targets[way]}
                    )
                yield
        for half in range(2):
            for way in range(2):
                copies[3 if half == way else 2, half, way].wait_recv()

    def scatter_steps(index, total):
        copies = {}
        for step in range(4):
            for half in range(2):
                for way in range(2):
                    length = 4 if half == way else 3
                    if step >= length:
                        continue
                    shift = length - step if way == 0 else RING - length + step
                    spot = (index, slab_rows(ring_device((place + shift) % RING), half))
                    spots = (index, step, half, way)
                    if step:
                        copies[step - 1, half, way].wait_recv()
                        come = k.arrived[index, step - 1, half, way].astype(wide)
                        k.leaving[spots] = (come + k.grads[spot].astype(wide)).astype(low)
                        source = k.leaving.at[spots]
                    else:
                        source = k.grads.at[spot]
                    copies[step, half, way] = send(
                        source, k.arrived.at[spots], k.s_send.at[spots], k.s_recv.at[spots], {"dp": targets[way]}
                    )
                yield
        for half in range(2):
            mine = k.grads[index, slab_rows(me, half)].astype(wide)
            for way in range(2):
                last = 3 if half == way else 2
                copies[last, half, way].wait_recv()
                mine += k.arrived[index, last, half, way].astype(wide)
            total[half * piece : (half + 1) * piece] = mine

    wire = []

    def poll(count=1):
        for turn in range(count):
            while wire and next(wire[0], "done") == "done":
                wire.pop(0)

    def finish(plan):
        for turn in plan:
            pass

    loads = [
        pltpu.make_async_copy(source, target, k.load_sem.at[spot])
        for spot, (source, target) in enumerate(
            (
                (k.inw_hbm, k.inw),
                (k.outw_hbm, k.outw),
                (k.tokens_hbm, k.tokens),
                (k.bias_hbm, k.bias),
                (k.norm_hbm, k.norm),
                (k.cot_hbm, k.cot),
            )
        )
    ]
    for load in loads:
        load.start()
    barrier = pltpu.get_barrier_semaphore()
    greeted = [{"dp": (me + shift) % RING} for shift in range(1, RING)]
    greeted += [{"tensor": partner}, {"tensor": across}]
    for device in greeted:
        pl.semaphore_signal(barrier, inc=1, device_id=device, device_id_type=MESH)
    loads[0].wait()
    loads[1].wait()
    mine = pl.ds(pl.multiple_of(me * slab, slab), slab)

    def lower(index, first, blocks):
        for place_at, block in enumerate(blocks):
            start = (first + place_at) * group
            k.full[index, mine, start : start + group] = block.astype(low)

    lower(ATTN, 0, [k.inw[spot] for spot in range(3)] + [k.outw[0].T])
    pl.semaphore_wait(barrier, len(greeted))
    gather_attn, gather_up, gather_down = [gather_steps(index) for index in range(3)]
    next(gather_attn)
    next(gather_attn)
    lower(UP, 0, [k.inw[3 + spot] for spot in range(4)])
    next(gather_up)
    next(gather_attn)
    next(gather_attn)
    lower(DOWN, 0, [k.outw[1 + spot].T for spot in range(4)])
    next(gather_up)
    next(gather_attn)
    next(gather_attn)
    for load in loads[2:]:
        load.wait()
    k.qkv_bias[...] = jnp.zeros_like(k.qkv_bias)
    k.qkv_bias[:, :group] = k.bias[0:1]
    k.qkv_bias[:, 2 * group : 3 * group] = k.bias[1:2]
    for spot in range(4):
        k.up_bias[:, spot * group : (spot + 1) * group] = k.bias[2 + spot : 3 + spot]
    k.tokens_t[...] = k.tokens[...].T
    next(gather_attn)
    next(gather_attn)
    next(gather_up)
    next(gather_down)
    finish(gather_attn)
    wire.extend([gather_up, gather_down])
    poll()

    def project(step, carry):
        spot = pl.ds(pl.multiple_of(step * 256, 256), 256)
        qkv = dot_nn(k.tokens[spot], k.full[ATTN]) + k.qkv_bias[...]
        for head in range(HEADS_HERE):
            start = head * HDIM
            k.query[head, spot] = (qkv[:, start : start + HDIM].astype(low) * HDIM**-0.5).astype(low)
            start += group
            k.key[head, spot] = qkv[:, start : start + HDIM].astype(low)
            start += group
            k.value[head, spot] = qkv[:, start : start + HDIM].astype(low)
        return carry

    lax.fori_loop(0, rows // 256, project, 0)
    poll()
    length = k.lengths[0]
    usable = lax.broadcasted_iota(jnp.int32, (rows, 256), 0) < length
    for head in range(HEADS_HERE):
        k.value_t[head] = k.value[head].T
        k.key_t[head] = (k.key[head] * HDIM**-0.5).astype(low).T
    for head in range(HEADS_HERE):

        def attend(step, carry, head=head):
            spot = pl.ds(pl.multiple_of(step * 256, 256), 256)
            scores = jnp.where(usable, dot_nt(k.key[head], k.query[head, spot]), masked_score)
            highest = jnp.max(scores, 0, keepdims=True)
            raised = jnp.exp(scores - highest)
            probs = raised * (1.0 / jnp.sum(raised, 0, keepdims=True))
            k.probs[head, :, spot] = probs
            mixed = dot_nn(k.value_t[head], probs.astype(low))
            k.mixed_t[head * HDIM : (head + 1) * HDIM, spot] = mixed.astype(low)
            return carry

        lax.fori_loop(0, rows // 256, attend, 0)
        poll()
    k.mixed[...] = k.mixed_t[...].T

    def chunk_steps(chunk):
        all_rows = pl.ds(chunk * span, span)
        own_rows = pl.ds(pl.multiple_of(chunk * span + core * own, own), own)
        other_rows = pl.ds(pl.multiple_of(chunk * span + (1 - core) * own, own), own)

        def send_near(which):
            spots = (which, chunk)
            return send(
                k.part.at[which, other_rows],
                k.near.at[spots],
                k.near_send.at[spots],
                k.near_recv.at[spots],
                {"tensor": partner},
            )

        def send_far(which, copy):
            spots = (which, chunk)
            copy.wait_recv()
            both = k.near[spots].astype(wide) + k.part[which, own_rows].astype(wide)
            k.chip[spots] = both.astype(low)
            return send(
                k.chip.at[spots], k.far.at[spots], k.far_send.at[spots], k.far_recv.at[spots], {"tensor": across}
            )

        def take_far(which, copy):
            copy.wait_recv()
            return k.chip[which, chunk].astype(wide) + k.far[which, chunk].astype(wide)

        def trade(which, ref):
            spots = (which, chunk)
            return send(
                ref.at[own_rows], ref.at[own_rows], k.ex_send.at[spots], k.ex_recv.at[spots], {"tensor": partner}
            )

        k.part[SUM_ATTN, all_rows] = dot_nt(k.mixed[all_rows], k.full[ATTN, :, 3 * group :]).astype(low)
        copy = send_near(SUM_ATTN)
        yield
        copy = send_far(SUM_ATTN, copy)
        yield
        attn = take_far(SUM_ATTN, copy)
        normed, inverse = normalize(k.tokens[own_rows].astype(wide) + attn + k.norm[0:1])
        k.normed1[chunk] = normed
        k.inverse1[chunk] = inverse
        hidden = normed * k.norm[1:2] + k.norm[2:3]
        k.hidden[chunk] = hidden
        k.hidden_low[own_rows] = hidden.astype(low)
        copy = trade(EX_HIDDEN, k.hidden_low)
        yield
        copy.wait_recv()
        pre = dot_nn(k.hidden_low[all_rows], k.full[UP]) + k.up_bias[...]
        below = 0.5 * (1.0 + lax.erf(pre * root_half))
        k.act[all_rows] = (pre * below).astype(low)
        k.slope[all_rows] = below + pre * jnp.exp(-0.5 * pre * pre) * normal_peak
        yield
        k.part[SUM_FFN, all_rows] = dot_nt(k.act[all_rows], k.full[DOWN]).astype(low)
        copy = send_near(SUM_FFN)
        yield
        copy = send_far(SUM_FFN, copy)
        yield
        ffn = take_far(SUM_FFN, copy)
        normed, inverse = normalize(k.hidden[chunk] + ffn + k.norm[3:4])
        k.out[own_rows] = (normed * k.norm[4:5] + k.norm[5:6]).astype(low)
        out_copy = trade(EX_OUT, k.out)
        positions = lax.broadcasted_iota(jnp.int32, (own, 1), 0) + (chunk * span + core * own)
        dout = k.cot[own_rows].astype(wide) * (positions < length).astype(wide)
        dres2 = norm_back(dout, normed, inverse, k.norm[4:5])
        k.dres2[chunk] = dres2
        k.dres2_low[own_rows] = dres2.astype(low)
        two_copy = trade(EX_TWO, k.dres2_low)
        k.norm_acc[chunk, 3:4] = column_sum(dres2)
        k.norm_acc[chunk, 4:5] = column_sum(dout * normed)
        k.norm_acc[chunk, 5:6] = column_sum(dout)
        k.norm_acc[chunk, 6:8] = jnp.zeros((2, width), wide)
        yield
        two_copy.wait_recv()
        dpre = dot_nn(k.dres2_low[all_rows], k.full[DOWN]) * k.slope[all_rows]
        k.bias_acc[chunk] = column_sum(dpre)
        k.dpre_low[all_rows] = dpre.astype(low)
        k.part[SUM_BACK, all_rows] = dot_nt(k.dpre_low[all_rows], k.full[UP]).astype(low)
        copy = send_near(SUM_BACK)
        yield
        copy = send_far(SUM_BACK, copy)
        yield
        dhidden = k.dres2[chunk] + take_far(SUM_BACK, copy)
        normed = k.normed1[chunk]
        dres1 = norm_back(dhidden, normed, k.inverse1[chunk], k.norm[1:2])
        k.dres1[chunk] = dres1
        k.dres1_low[own_rows] = dres1.astype(low)
        copy = trade(EX_ONE, k.dres1_low)
        k.norm_acc[chunk, 0:1] = column_sum(dres1)
        k.norm_acc[chunk, 1:2] = column_sum(dhidden * normed)
        k.norm_acc[chunk, 2:3] = column_sum(dhidden)
        yield
        copy.wait_recv()
        dmix = dot_nn(k.dres1_low[all_rows], k.full[ATTN, :, 3 * group :]).astype(low)
        for head in range(HEADS_HERE):
            k.dmix[head, all_rows] = dmix[:, head * HDIM : (head + 1) * HDIM]
        yield
        k.part[SUM_INPUT, all_rows] = dot_nt(k.dqkv[all_rows], k.full[ATTN]).astype(low)
        copy = send_near(SUM_INPUT)
        yield
        copy = send_far(SUM_INPUT, copy)
        yield
        total = k.dres1[chunk] + take_far(SUM_INPUT, copy)
        k.gin[own_rows] = total.astype(low)
        copy = trade(EX_INPUT, k.gin)
        yield
        copy.wait_recv()
        out_copy.wait_recv()

    chunks = [chunk_steps(chunk) for chunk in range(CHUNKS)]

    def stage(polls=()):
        for chunk, plan in enumerate(chunks):
            next(plan, None)
            poll(polls[chunk] if chunk < len(polls) else 0)

    def grad_tile(index, left_t, right):
        def body(step, carry):
            spot = pl.ds(pl.multiple_of(step * 256, 256), 256)
            k.grads[index, spot] = dot_nn(left_t[spot], right[...]).astype(low)
            return carry

        lax.fori_loop(0, width // 256, body, 0)

    stage()
    stage((0, 0, 0, 1))
    stage((0, 1, 0, 1))
    finish(gather_up)
    stage((0, 1, 0, 1))
    finish(gather_down)
    stage()
    stage()
    stage()
    stage()
    k.turned[...] = k.dres2_low[...].T
    grad_tile(DOWN, k.turned, k.act)
    scatter_down = scatter_steps(DOWN, k.tot2)
    scatter_up = scatter_steps(UP, k.tot1)
    scatter_attn = scatter_steps(ATTN, k.tot0)
    next(scatter_down)
    next(scatter_down)
    stage()
    k.turned[...] = k.hidden_low[...].T
    grad_tile(UP, k.turned, k.dpre_low)
    next(scatter_up)

    def mixed_wire():
        for plan, count in (
            (scatter_down, 2),
            (scatter_up, 1),
            (scatter_down, 2),
            (scatter_up, 1),
            (scatter_down, 9),
            (scatter_up, 9),
        ):
            for turn in range(count):
                if next(plan, "done") == "done":
                    break
                yield

    wire.append(mixed_wire())
    poll()
    stage((0, 1, 0, 1))
    stage((0, 1, 0, 1))
    k.dqkv[:, 3 * group :] = jnp.zeros((rows, width - 3 * group), low)
    k.small[...] = jnp.zeros_like(k.small)
    for head in range(HEADS_HERE):
        start = head * HDIM
        dkey, dvalue = 0.0, 0.0
        for step in range(rows // 256):
            spot = pl.ds(step * 256, 256)
            dprob = dot_nt(k.value[head], k.dmix[head, spot])
            probs = k.probs[head, :, spot]
            total = jnp.sum(probs * dprob, 0, keepdims=True)
            dscore = (probs * (dprob - total)).astype(low)
            k.dquery_t[start : start + HDIM, spot] = dot_nn(k.key_t[head], dscore)
            dkey += dot_nn(dscore, k.query[head, spot])
            dvalue += dot_nn(probs.astype(low), k.dmix[head, spot])
        k.dqkv[:, group + start : group + start + HDIM] = dkey.astype(low)
        k.dqkv[:, 2 * group + start : 2 * group + start + HDIM] = dvalue.astype(low)
        k.small[1:2, 384 + start : 384 + start + HDIM] = column_sum(dvalue)
        poll(2)
    dquery = k.dquery_t[...].T
    k.dqkv[:, :group] = dquery.astype(low)
    k.small[0:1, 384 : 384 + group] = column_sum(dquery)
    stage()
    grad_tile(ATTN, k.tokens_t, k.dqkv)
    k.turned[...] = k.dres1_low[...].T
    k.grads[ATTN, :, 3 * group :] = dot_nn(k.turned[...], k.mixed[...]).astype(low)
    next(scatter_attn)
    next(scatter_attn)
    stage()
    norm_total = k.norm_acc[0]
    bias_total = k.bias_acc[0]
    for chunk in range(1, CHUNKS):
        norm_total += k.norm_acc[chunk]
        bias_total += k.bias_acc[chunk]
    half_width = width // 2
    k.norm_half[0] = norm_total[:, :half_width]
    k.norm_half[1] = norm_total[:, half_width:]
    pair = send(
        k.norm_half.at[1 - core], k.norm_in, k.pair_send.at[0], k.pair_recv.at[0], {"tensor": partner}
    )
    for spot in range(4):
        k.small[2 + spot : 3 + spot, 384 : 384 + group] = bias_total[:, spot * group : (spot + 1) * group]
    pair.wait_recv()
    k.small[:, :half_width] = k.norm_half[core] + k.norm_in[...]
    shared = [
        send(
            k.small,
            k.slots.at[me],
            k.dp_send.at[shift - 1],
            k.dp_recv.at[shift - 1],
            {"dp": (me + shift) % RING},
        )
        for shift in range(1, RING)
    ]
    k.slots[me] = k.small[...]
    while wire:
        poll()
    finish(scatter_up)
    next(scatter_attn)
    stage()
    next(scatter_attn)
    stage()
    next(scatter_attn)
    for copy in shared:
        copy.wait_recv()
    small_total = k.slots[0]
    for index in range(1, RING):
        small_total += k.slots[index]
    k.bias_out[...] = small_total[:, 384:640]
    k.norm_fin[core] = small_total[:, :half_width]
    pair = send(
        k.norm_fin.at[core], k.norm_fin.at[core], k.pair_send.at[1], k.pair_recv.at[1], {"tensor": partner}
    )
    next(scatter_attn)
    stage()
    finish(scatter_attn)
    pair.wait_recv()
    k.norm_out[...] = k.norm_fin[...]
    for copy in sent:
        copy.wait_send()


def run_layer(tokens, cotangent, lengths, in_weight, out_weight, in_bias, norm_vec):
    rows, width = tokens.shape
    slab, group = in_weight.shape[1:]
    scratch = scratch_list(rows, width, slab, group)
    names = INPUTS + OUTPUTS + tuple(scratch)
    anywhere = pl.BlockSpec(memory_space=pl.ANY)
    inside = pl.BlockSpec(memory_space=pltpu.VMEM)
    scalar = pl.BlockSpec(memory_space=pltpu.SMEM)
    total = jax.ShapeDtypeStruct((slab, width), jnp.float32)
    like = jax.ShapeDtypeStruct((rows, width), jnp.bfloat16)
    return pl.pallas_call(
        functools.partial(layer_kernel, names),
        out_shape=(
            like,
            like,
            total,
            total,
            total,
            jax.ShapeDtypeStruct((2, 8, width // 2), jnp.float32),
            jax.ShapeDtypeStruct((8, 256), jnp.float32),
        ),
        in_specs=[anywhere, anywhere, scalar] + [anywhere] * 4,
        out_specs=(inside,) * len(OUTPUTS),
        scratch_shapes=list(scratch.values()),
        compiler_params=pltpu.CompilerParams(
            collective_id=0, has_side_effects=True, vmem_limit_bytes=56 * 2**20
        ),
        name="layer",
    )(tokens, cotangent, lengths, in_weight, out_weight, in_bias, norm_vec)


def scatter_plain(grads):
    share = lax.psum_scatter(grads, "dp", scatter_dimension=0, tiled=True)
    return share.astype(jnp.float32)


def matmul(left_op, right_op):
    return jnp.dot(left_op, right_op, preferred_element_type=jnp.float32)


def inner_rows(left_op, right_op):
    return lax.dot_general(
        left_op, right_op, (((0,), (0,)), ((), ())), preferred_element_type=jnp.float32
    )


def times_transposed(left_op, right_op):
    return lax.dot_general(
        left_op, right_op, (((1,), (1,)), ((), ())), preferred_element_type=jnp.float32
    )


def layer_norm(summed_rows, gain_vec, shift_vec):
    center = jnp.mean(summed_rows, -1, keepdims=True)
    offset = summed_rows - center
    inverse = lax.rsqrt(jnp.mean(offset * offset, -1, keepdims=True) + norm_eps)
    normed = offset * inverse
    return (normed * gain_vec + shift_vec, normed, inverse)


def norm_back(upstream, normed, inverse, gain_vec):
    scaled = upstream * gain_vec
    return inverse * (
        scaled
        - jnp.mean(scaled, -1, keepdims=True)
        - normed * jnp.mean(scaled * normed, -1, keepdims=True)
    )


def gelu_value(pre_act):
    return 0.5 * pre_act * (1.0 + jax.scipy.special.erf(pre_act * root_half))


def gelu_slope(pre_act):
    return (
        0.5 * (1.0 + jax.scipy.special.erf(pre_act * root_half))
        + pre_act * jnp.exp(-0.5 * pre_act * pre_act) * normal_peak
    )


def score_block(query_heads, key_heads, length):
    seq_len = query_heads.shape[0]
    scale_factor = query_heads.shape[-1] ** (-0.5)
    scores = (
        jnp.einsum("qhe,khe->hqk", query_heads, key_heads, preferred_element_type=jnp.float32)
        * scale_factor
    )
    usable = lax.broadcasted_iota(jnp.int32, (1, 1, seq_len), 2) < length
    return jnp.where(usable, scores, masked_score)


def attend_forward(operands):
    query_heads, key_heads, value_heads, length = operands
    scores = score_block(query_heads, key_heads, length)
    highest = jnp.max(scores, -1, keepdims=True)
    log_total = highest + jnp.log(jnp.sum(jnp.exp(scores - highest), -1, keepdims=True))
    probs_low = jnp.exp(scores - log_total).astype(jnp.bfloat16)
    mixed_heads = jnp.einsum(
        "hqk,khe->qhe", probs_low, value_heads, preferred_element_type=jnp.float32
    )
    return (mixed_heads.astype(jnp.bfloat16), log_total)


def attend_backward(operands):
    query_heads, key_heads, value_heads, grad_heads, log_total, length = operands
    scale_factor = query_heads.shape[-1] ** (-0.5)
    scores = score_block(query_heads, key_heads, length)
    probs = jnp.exp(scores - log_total)
    probs_low = probs.astype(jnp.bfloat16)
    grad_probs = jnp.einsum(
        "qhe,khe->hqk", grad_heads, value_heads, preferred_element_type=jnp.float32
    )
    row_dot = jnp.sum(probs * grad_probs, -1, keepdims=True)
    grad_scores = (probs * (grad_probs - row_dot) * scale_factor).astype(jnp.bfloat16)
    grad_query = jnp.einsum(
        "hqk,khe->qhe", grad_scores, key_heads, preferred_element_type=jnp.float32
    )
    grad_keys = jnp.einsum(
        "hqk,qhe->khe", grad_scores, query_heads, preferred_element_type=jnp.float32
    )
    grad_values = jnp.einsum(
        "hqk,qhe->khe", probs_low, grad_heads, preferred_element_type=jnp.float32
    )
    return (grad_query, grad_keys, grad_values)


def adam_update(param, grad, moments, decay):
    first = beta_first * moments[0] + (1.0 - beta_first) * grad
    second = beta_second * moments[1] + (1.0 - beta_second) * grad * grad
    first_hat = first / (1.0 - beta_first**step_count)
    second_hat = second / (1.0 - beta_second**step_count)
    new_param = param - learn_rate * (first_hat / (jnp.sqrt(second_hat) + adam_eps) + decay * param)
    return (new_param, jnp.stack([first, second]))


def adam_store(param, grad, moments, decay, new_param, new_moments):
    first = beta_first * moments[0] + (1.0 - beta_first) * grad
    second = beta_second * moments[1] + (1.0 - beta_second) * grad * grad
    first_hat = first / (1.0 - beta_first**step_count)
    second_hat = second / (1.0 - beta_second**step_count)
    step = first_hat / (jnp.sqrt(second_hat) + adam_eps) + decay * param
    new_param[...] = param - learn_rate * step
    new_moments[0] = first
    new_moments[1] = second


def adam_kernel(tot0, tot1, tot2, norm_ref, bias_ref, *refs):
    params, moments = refs[:4], refs[4:8]
    grads, new_params, new_moments = refs[8:12], refs[12:16], refs[16:20]
    width = params[0].shape[2]
    for index in range(12):
        source, place = (tot0, tot1, tot2)[index // 4], index % 4
        grad = source[:, place * width : (place + 1) * width]
        if index == 3 or index >= 8:
            group, spot, grad = 1, (0 if index == 3 else index - 7), grad.T
        else:
            group, spot = 0, (index if index < 3 else index - 1)
        grads[group][spot] = grad
        adam_store(
            params[group][spot],
            grad,
            (moments[group][0, spot], moments[group][1, spot]),
            weight_decay,
            new_params[group].at[spot],
            new_moments[group].at[:, spot],
        )
    norm_grad = jnp.concatenate([norm_ref[0, :6], norm_ref[1, :6]], 1)
    for group, grad in ((2, bias_ref[:6, :width]), (3, norm_grad)):
        grads[group][...] = grad
        adam_store(
            params[group][...], grad, moments[group], 0.0, new_params[group], new_moments[group]
        )


def update_here(totals, params, moments):
    inside = pl.BlockSpec(memory_space=pltpu.VMEM)
    shapes = [jax.ShapeDtypeStruct(a.shape, jnp.float32) for a in params + params + moments]
    return pl.pallas_call(
        adam_kernel,
        out_shape=tuple(shapes),
        in_specs=[inside] * (len(totals) + 8),
        out_specs=(inside,) * 12,
        name="adam",
    )(*totals, *params, *moments)


def update_plain(share, rest, small, params, moments):
    group_width, width = params[0].shape[2], params[3].shape[1]
    total = jnp.concatenate([share, rest], 1)
    blocks = [total[:, k * group_width : (k + 1) * group_width] for k in range(12)]
    grads = (
        jnp.stack(blocks[:3] + blocks[4:8]),
        jnp.stack([blocks[3]] + blocks[8:]).swapaxes(1, 2),
        small[:6, width : width + group_width],
        small[:6, :width],
    )
    decays = (weight_decay, weight_decay, 0.0, 0.0)
    news = [adam_update(*group) for group in zip(params, grads, moments, decays)]
    return grads + tuple(n[0] for n in news) + tuple(n[1] for n in news)


def plain_layer(
    tokens,
    cotangent,
    lengths,
    in_weight,
    out_weight,
    in_bias,
    norm_vec,
    in_moments,
    out_moments,
    bias_moments,
    norm_moments,
):
    seq_count, seq_len, width = tokens.shape
    row_count = seq_count * seq_len
    in_low = in_weight.astype(jnp.bfloat16)
    out_low = out_weight.astype(jnp.bfloat16).swapaxes(1, 2)
    share = jnp.concatenate(list(in_low[:3]) + [out_low[0]], 1)
    rest = jnp.concatenate(list(in_low[3:]) + list(out_low[1:]), 1)
    first_full = lax.all_gather(share, "dp", axis=0, tiled=True)
    second_full = lax.all_gather(rest, "dp", axis=0, tiled=True)
    group_width = in_weight.shape[2]
    heads_here = group_width // HDIM
    w_qkv = first_full[:, : 3 * group_width]
    w_proj = first_full[:, 3 * group_width :]
    bias_up = in_bias[2:6].reshape(1, 4 * group_width)

    def split_heads(flat_rows):
        return flat_rows.reshape(seq_count, seq_len, heads_here, HDIM)

    flat_tokens = tokens.reshape(row_count, width)
    qkv = matmul(flat_tokens, w_qkv)
    query = (qkv[:, :group_width] + in_bias[0]).astype(jnp.bfloat16)
    keys_low = qkv[:, group_width : 2 * group_width].astype(jnp.bfloat16)
    values_low = (qkv[:, 2 * group_width :] + in_bias[1]).astype(jnp.bfloat16)
    mixed_heads, log_total = lax.map(
        attend_forward,
        (split_heads(query), split_heads(keys_low), split_heads(values_low), lengths),
    )
    mixed_flat = mixed_heads.reshape(row_count, group_width)
    attn_part = times_transposed(mixed_flat, w_proj).astype(jnp.bfloat16)
    attn_out = lax.psum(attn_part, "tensor")
    w_up = second_full[:, : 4 * group_width]
    w_down = second_full[:, 4 * group_width :]
    hidden, normed_one, inverse_one = layer_norm(
        flat_tokens.astype(jnp.float32) + attn_out.astype(jnp.float32) + norm_vec[0], norm_vec[1], norm_vec[2]
    )
    hidden_low = hidden.astype(jnp.bfloat16)
    pre_act = matmul(hidden_low, w_up) + bias_up
    act_low = gelu_value(pre_act).astype(jnp.bfloat16)
    ffn_part = times_transposed(act_low, w_down).astype(jnp.bfloat16)
    ffn_out = lax.psum(ffn_part, "tensor").astype(jnp.float32)
    out_rows, normed_two, inverse_two = layer_norm(
        hidden + ffn_out + norm_vec[3], norm_vec[4], norm_vec[5]
    )
    positions = lax.broadcasted_iota(jnp.int32, (seq_count, seq_len), 1)
    live_rows = (positions < lengths[:, None]).astype(jnp.float32).reshape(row_count, 1)
    grad_out = cotangent.reshape(row_count, width).astype(jnp.float32) * live_rows
    grad_two = norm_back(grad_out, normed_two, inverse_two, norm_vec[4])
    grad_two_low = grad_two.astype(jnp.bfloat16)
    grad_down = inner_rows(grad_two_low, act_low).astype(jnp.bfloat16)
    grad_act = matmul(grad_two_low, w_down)
    grad_pre = grad_act * gelu_slope(pre_act)
    grad_pre_low = grad_pre.astype(jnp.bfloat16)
    grad_up = inner_rows(hidden_low, grad_pre_low).astype(jnp.bfloat16)
    rest_grads = jnp.concatenate([grad_up, grad_down], 1)
    back_part = times_transposed(grad_pre_low, w_up).astype(jnp.bfloat16)
    back_sum = lax.psum(back_part, "tensor")
    grad_hidden = grad_two + back_sum.astype(jnp.float32)
    grad_one = norm_back(grad_hidden, normed_one, inverse_one, norm_vec[1])
    grad_one_low = grad_one.astype(jnp.bfloat16)
    grad_proj = inner_rows(grad_one_low, mixed_flat).astype(jnp.bfloat16)
    grad_mixed = matmul(grad_one_low, w_proj).astype(jnp.bfloat16)
    grad_query, grad_keys, grad_values = lax.map(
        attend_backward,
        (
            split_heads(query),
            split_heads(keys_low),
            split_heads(values_low),
            split_heads(grad_mixed),
            log_total,
            lengths,
        ),
    )
    grad_query = grad_query.reshape(row_count, group_width)
    grad_keys = grad_keys.reshape(row_count, group_width)
    grad_values = grad_values.reshape(row_count, group_width)
    qkv_grad_low = jnp.concatenate([grad_query, grad_keys, grad_values], 1).astype(jnp.bfloat16)
    input_part = times_transposed(qkv_grad_low, w_qkv).astype(jnp.bfloat16)
    grad_qkv = inner_rows(flat_tokens, qkv_grad_low).astype(jnp.bfloat16)
    first_grads = jnp.concatenate([grad_qkv, grad_proj], 1)
    bias_rows = jnp.concatenate(
        [jnp.sum(grad_query, 0), jnp.sum(grad_values, 0), jnp.sum(grad_pre, 0)]
    ).reshape(6, group_width)
    norm_rows = jnp.stack(
        [
            jnp.sum(grad_one, 0),
            jnp.sum(grad_hidden * normed_one, 0),
            jnp.sum(grad_hidden, 0),
            jnp.sum(grad_two, 0),
            jnp.sum(grad_out * normed_two, 0),
            jnp.sum(grad_out, 0),
        ]
    )
    small = jnp.pad(jnp.concatenate([norm_rows, bias_rows], 1), ((0, 2), (0, 64)))
    share_total = scatter_plain(first_grads)
    rest_total = scatter_plain(rest_grads)
    input_sum = lax.psum(input_part, "tensor")
    small_total = lax.psum(small, "dp")
    grad_input = grad_one + input_sum.astype(jnp.float32)
    params = (in_weight, out_weight, in_bias, norm_vec)
    moments = (in_moments, out_moments, bias_moments, norm_moments)
    updates = update_plain(share_total, rest_total, small_total, params, moments)
    output = out_rows.astype(jnp.bfloat16).reshape(seq_count, seq_len, width)
    grad_tokens = grad_input.astype(jnp.bfloat16).reshape(seq_count, seq_len, width)
    return (
        output,
        grad_tokens,
    ) + tuple(updates)


def local(*operands):
    tokens, cotangent, lengths, in_weight, out_weight, in_bias, norm_vec = operands[:7]
    ring = lax.axis_size("dp") == RING and lax.axis_size("tensor") == 4
    if not ring or tokens.shape[0] != 1:
        return plain_layer(*operands)
    out, grad_tokens, *totals = run_layer(
        tokens[0], cotangent[0], lengths, in_weight, out_weight, in_bias, norm_vec
    )
    updates = update_here(tuple(totals), operands[3:7], operands[7:])
    return (out[None], grad_tokens[None]) + tuple(updates)


def solution(mesh):
    in_specs = (
        P("dp", None, None),
        P("dp", None, None),
        P("dp"),
        P(None, "dp", "tensor"),
        P(None, "tensor", "dp"),
        P(None, "tensor"),
        P(),
        P(None, None, "dp", "tensor"),
        P(None, None, "tensor", "dp"),
        P(None, None, "tensor"),
        P(),
    )
    out_specs = (
        P("dp", None, None),
        P("dp", None, None),
        P(None, "dp", "tensor"),
        P(None, "tensor", "dp"),
        P(None, "tensor"),
        P(),
        P(None, "dp", "tensor"),
        P(None, "tensor", "dp"),
        P(None, "tensor"),
        P(),
        P(None, None, "dp", "tensor"),
        P(None, None, "tensor", "dp"),
        P(None, None, "tensor"),
        P(),
    )
    return jax.shard_map(local, mesh=mesh, in_specs=in_specs, out_specs=out_specs, check_vma=False)
```

```python
import functools

import jax
import jax.numpy as jnp
from jax import lax
from jax.experimental import pallas as pl
from jax.experimental.pallas import tpu as pltpu
from jax.sharding import PartitionSpec as P

HDIM = 64


norm_eps = 1e-12
masked_score = -1e30
learn_rate = 0.005
beta_first = 0.9
beta_second = 0.999
adam_eps = 1e-08
weight_decay = 0.01
step_count = 2.0
root_half = 0.7071067811865476
normal_peak = 0.3989422804014327


RING = 8
CHUNKS = 4
PIECE_TIME = 1.78
LINK_DELAY = {"near": 1.8, "far": 1.4, 0: 1.8, 1: 1.8}
FILL_LIMIT = (0.5, 3.5, 5.0)
SCATTER_LIMIT = 99.0
COST = [c * 3.6 / CHUNKS for c in (0.2, 0.1, 0.25, 0.6, 0.3, 0.45, 0.6, 0.35, 0.2, 0.3, 0.15)]
HEADS_HERE = 3
MESH = pl.DeviceIdType.MESH
ATTN, UP, DOWN = 0, 1, 2
SUM_ATTN, SUM_FFN, SUM_BACK, SUM_INPUT = 0, 1, 2, 3
EX_HIDDEN, EX_OUT, EX_TWO, EX_ONE, EX_INPUT = 0, 1, 2, 3, 4


def ring_place(index):
    depth, side = index // 2, index % 2
    return depth + side * (RING - 1 - 2 * depth)


def ring_device(place):
    side = place // (RING // 2)
    depth = place + side * (RING - 1 - 2 * place)
    return 2 * depth + side


def dot_nn(left_op, right_op):
    return jnp.dot(left_op, right_op, preferred_element_type=jnp.float32)


def dot_nt(left_op, right_op):
    return lax.dot_general(
        left_op, right_op, (((1,), (1,)), ((), ())), preferred_element_type=jnp.float32
    )


def normalize(rows):
    center = jnp.mean(rows, -1, keepdims=True)
    offset = rows - center
    inverse = lax.rsqrt(jnp.mean(offset * offset, -1, keepdims=True) + norm_eps)
    return offset * inverse, inverse


def column_sum(rows):
    return jnp.sum(rows, 0, keepdims=True)


INPUTS = ("tokens_hbm", "cot_hbm", "lengths", "inw_hbm", "outw_hbm", "bias_hbm", "norm_hbm")
OUTPUTS = ("out_hbm", "gin_hbm", "tot0", "tot1", "tot2", "norm_out", "bias_out")


def scratch_list(rows, width, slab, group):
    own = rows // (2 * CHUNKS)
    piece = slab // 2
    low, wide = jnp.bfloat16, jnp.float32
    dma = pltpu.SemaphoreType.DMA
    vmem = pltpu.VMEM
    heads = (HEADS_HERE, rows, HDIM)
    turned = (HEADS_HERE, HDIM, rows)
    return {
        "tokens": vmem((rows, width), low),
        "out": vmem((rows, width), low),
        "gin": vmem((rows, width), low),
        "store_sem": dma((2, CHUNKS)),
        "cot": vmem((rows, width), low),
        "inw": vmem((7, slab, group), wide),
        "outw": vmem((5, group, slab), wide),
        "bias": vmem((6, group), wide),
        "norm": vmem((6, width), wide),
        "full": vmem((3, width, width), low),
        "grads": vmem((3, width, width), low),
        "arrived": vmem((3, 4, 2, 2, piece, width), low),
        "leaving": vmem((3, 4, 2, 2, piece, width), low),
        "tokens_t": vmem((width, rows), low),
        "qkv_bias": vmem((1, width), wide),
        "up_bias": vmem((1, width), wide),
        "query": vmem(heads, low),
        "key": vmem(heads, low),
        "value": vmem(heads, low),
        "dmix": vmem(heads, low),
        "key_t": vmem(turned, low),
        "value_t": vmem(turned, low),
        "probs": vmem((HEADS_HERE, rows, rows), wide),
        "mixed_t": vmem((group, rows), low),
        "mixed": vmem((rows, group), low),
        "dquery_t": vmem((group, rows), wide),
        "dqkv": vmem((rows, width), low),
        "part": vmem((4, rows, width), low),
        "near": vmem((4, CHUNKS, own, width), low),
        "chip": vmem((4, CHUNKS, own, width), low),
        "far": vmem((4, CHUNKS, own, width), low),
        "hidden": vmem((CHUNKS, own, width), wide),
        "normed1": vmem((CHUNKS, own, width), wide),
        "inverse1": vmem((CHUNKS, own, 1), wide),
        "dres2": vmem((CHUNKS, own, width), wide),
        "dres1": vmem((CHUNKS, own, width), wide),
        "hidden_low": vmem((rows, width), low),
        "dres2_low": vmem((rows, width), low),
        "dres1_low": vmem((rows, width), low),
        "act": vmem((rows, width), low),
        "slope": vmem((rows, width), wide),
        "dpre_low": vmem((rows, width), low),
        "norm_acc": vmem((CHUNKS, 8, width), wide),
        "bias_acc": vmem((CHUNKS, 1, width), wide),
        "norm_half": vmem((2, 8, width // 2), wide),
        "norm_in": vmem((8, width // 2), wide),
        "small": vmem((8, 640), wide),
        "norm_fin": vmem((2, 8, width // 2), wide),
        "turned": vmem((width, rows), low),
        "slots": vmem((RING, 8, 640), wide),
        "load_sem": dma((6,)),
        "g_send": dma((3, 4, 2, 2)),
        "g_recv": dma((3, 4, 2, 2)),
        "s_send": dma((3, 4, 2, 2)),
        "s_recv": dma((3, 4, 2, 2)),
        "near_send": dma((4, CHUNKS)),
        "near_recv": dma((4, CHUNKS)),
        "far_send": dma((4, CHUNKS)),
        "far_recv": dma((4, CHUNKS)),
        "ex_send": dma((5, CHUNKS)),
        "ex_recv": dma((5, CHUNKS)),
        "dp_send": dma((RING - 1,)),
        "dp_recv": dma((RING - 1,)),
        "pair_send": dma((2,)),
        "pair_recv": dma((2,)),
    }


class Names:
    pass


def layer_kernel(names, *refs):
    k = Names()
    for name, ref in zip(names, refs):
        setattr(k, name, ref)
    rows, width = k.tokens.shape
    group, slab = k.bias.shape[1], k.inw.shape[1]
    span = rows // CHUNKS
    own = span // 2
    piece = slab // 2
    low, wide = jnp.bfloat16, jnp.float32
    me, tensor = lax.axis_index("dp"), lax.axis_index("tensor")
    core = tensor % 2
    partner, across = tensor + 1 - 2 * core, (tensor + 2) % 4
    place = ring_place(me)
    targets = (ring_device((place + 1) % RING), ring_device((place + RING - 1) % RING))
    passed, stores, sent, done, free = [], [], [], set(), dict.fromkeys(("near", "far", 0, 1), 0.0)
    clock = [0.0]

    def send(source, target, send_sem, recv_sem, device, link, busy):
        copy = pltpu.make_async_remote_copy(
            src_ref=source,
            dst_ref=target,
            send_sem=send_sem,
            recv_sem=recv_sem,
            device_id=device,
            device_id_type=MESH,
        )
        copy.start()
        sent.append(copy)
        free[link] = max(free[link], clock[0]) + busy
        return copy, free[link] + LINK_DELAY[link]

    def run_all(plans):
        active = [[rank, plan, next(plan)] for rank, plan in plans]
        while active:
            best = None
            for item in active:
                rank, plan, (flags, flights, cost, gate) = item
                if any(flag not in done for flag in flags):
                    continue
                ready = max([clock[0]] + [flight[1] for flight in flights])
                if gate:
                    limit = gate[1] if gate[2] else FILL_LIMIT[min(len(passed) // 4, 2)]
                    ready = max(ready, free[gate[0]] - limit)
                if best is None or (ready, rank) < best[0]:
                    best = (ready, rank), item
            (ready, rank), item = best
            clock[0] = ready + item[2][2]
            item[2] = next(item[1], None)
            if item[2] is None:
                active.remove(item)

    def slab_rows(owner, half):
        return pl.ds(pl.multiple_of(owner * slab + half * piece, piece), piece)

    def gather_chain(index, half, way):
        length = 4 if half == way else 3
        flight = None
        for step in range(length):
            shift = RING - step if way == 0 else step
            spot = k.full.at[index, slab_rows(ring_device((place + shift) % RING), half)]
            spots = (index, step, half, way)
            gate = (way, 99.0, index == ATTN)
            if step:
                yield (), (flight,), 0.05, gate
                flight[0].wait_recv()
            else:
                yield (("own", index),), (), 0.05, gate
            flight = send(
                spot, spot, k.g_send.at[spots], k.g_recv.at[spots], {"dp": targets[way]}, way, PIECE_TIME
            )
        passed.append(index)
        yield (), (flight,), 0.02, None
        flight[0].wait_recv()
        done.add(("full", index, half, way))

    def all_of(index):
        return tuple(("full", index, half, way) for half in range(2) for way in range(2))

    def every(name):
        return tuple((name, chunk) for chunk in range(CHUNKS))

    ends = {}

    def scatter_chain(index, half, way):
        length = 4 if half == way else 3
        flight = None
        for step in range(length):
            shift = length - step if way == 0 else RING - length + step
            spot = (index, slab_rows(ring_device((place + shift) % RING), half))
            spots = (index, step, half, way)
            gate = (way, SCATTER_LIMIT, True)
            if step:
                yield (), (flight,), 0.08, gate
                flight[0].wait_recv()
                come = k.arrived[index, step - 1, half, way].astype(wide)
                k.leaving[spots] = (come + k.grads[spot].astype(wide)).astype(low)
                source = k.leaving.at[spots]
            else:
                yield (("grad", index),), (), 0.05, gate
                source = k.grads.at[spot]
            flight = send(
                source,
                k.arrived.at[spots],
                k.s_send.at[spots],
                k.s_recv.at[spots],
                {"dp": targets[way]},
                way,
                PIECE_TIME,
            )
        ends[index, half, way] = flight
        done.add(("end", index, half, way))

    def scatter_end(index, half, total):
        yield tuple(("end", index, half, way) for way in range(2)), (), 0.0, None
        yield (), tuple(ends[index, half, way] for way in range(2)), 0.1, None
        mine = k.grads[index, slab_rows(me, half)].astype(wide)
        for way in range(2):
            ends[index, half, way][0].wait_recv()
            mine += k.arrived[index, 3 if half == way else 2, half, way].astype(wide)
        total[half * piece : (half + 1) * piece] = mine

    loads = [
        pltpu.make_async_copy(source, target, k.load_sem.at[spot])
        for spot, (source, target) in enumerate(
            (
                (k.inw_hbm, k.inw),
                (k.outw_hbm, k.outw),
                (k.tokens_hbm, k.tokens),
                (k.bias_hbm, k.bias),
                (k.norm_hbm, k.norm),
                (k.cot_hbm, k.cot),
            )
        )
    ]
    for load in loads:
        load.start()
    barrier = pltpu.get_barrier_semaphore()
    greeted = [{"dp": (me + shift) % RING} for shift in range(1, RING)]
    greeted += [{"tensor": partner}, {"tensor": across}]
    for device in greeted:
        pl.semaphore_signal(barrier, inc=1, device_id=device, device_id_type=MESH)
    mine = pl.ds(pl.multiple_of(me * slab, slab), slab)

    def lower(index, first, blocks):
        for place_at, block in enumerate(blocks):
            start = (first + place_at) * group
            k.full[index, mine, start : start + group] = block.astype(low)
        done.add(("own", index))

    def prepare():
        yield (), (), 2.0, None
        loads[0].wait()
        loads[1].wait()
        lower(ATTN, 0, [k.inw[spot] for spot in range(3)] + [k.outw[0].T])
        pl.semaphore_wait(barrier, len(greeted))
        yield (), (), 0.4, None
        lower(UP, 0, [k.inw[3 + spot] for spot in range(4)])
        yield (), (), 0.6, None
        lower(DOWN, 0, [k.outw[1 + spot].T for spot in range(4)])
        yield (), (), 0.6, None
        for load in loads[2:]:
            load.wait()
        k.qkv_bias[...] = jnp.zeros_like(k.qkv_bias)
        k.qkv_bias[:, :group] = k.bias[0:1]
        k.qkv_bias[:, 2 * group : 3 * group] = k.bias[1:2]
        for spot in range(4):
            k.up_bias[:, spot * group : (spot + 1) * group] = k.bias[2 + spot : 3 + spot]
        k.dqkv[:, 3 * group :] = jnp.zeros((rows, width - 3 * group), low)
        k.small[...] = jnp.zeros_like(k.small)
        k.tokens_t[...] = k.tokens[...].T
        done.add("ready")

    def project(step, carry):
        spot = pl.ds(pl.multiple_of(step * 256, 256), 256)
        qkv = dot_nn(k.tokens[spot], k.full[ATTN]) + k.qkv_bias[...]
        for head in range(HEADS_HERE):
            start = head * HDIM
            k.query[head, spot] = (qkv[:, start : start + HDIM].astype(low) * HDIM**-0.5).astype(low)
            start += group
            k.key[head, spot] = qkv[:, start : start + HDIM].astype(low)
            start += group
            k.value[head, spot] = qkv[:, start : start + HDIM].astype(low)
        return carry

    length = k.lengths[0]

    def attention():
        yield all_of(ATTN) + ("ready",), (), 0.8, None
        lax.fori_loop(0, rows // 256, project, 0)
        yield (), (), 0.3, None
        usable = lax.broadcasted_iota(jnp.int32, (rows, 256), 0) < length
        for head in range(HEADS_HERE):
            k.value_t[head] = k.value[head].T
            k.key_t[head] = (k.key[head] * HDIM**-0.5).astype(low).T
        for head in range(HEADS_HERE):

            def attend(step, carry, head=head):
                spot = pl.ds(pl.multiple_of(step * 256, 256), 256)
                scores = jnp.where(usable, dot_nt(k.key[head], k.query[head, spot]), masked_score)
                highest = jnp.max(scores, 0, keepdims=True)
                raised = jnp.exp(scores - highest)
                probs = raised * (1.0 / jnp.sum(raised, 0, keepdims=True))
                k.probs[head, :, spot] = probs
                mixed = dot_nn(k.value_t[head], probs.astype(low))
                k.mixed_t[head * HDIM : (head + 1) * HDIM, spot] = mixed.astype(low)
                return carry

            yield (), (), 0.9, None
            lax.fori_loop(0, rows // 256, attend, 0)
        yield (), (), 0.15, None
        k.mixed[...] = k.mixed_t[...].T
        done.add("mixed")

    def chunk_steps(chunk):
        all_rows = pl.ds(chunk * span, span)
        own_rows = pl.ds(pl.multiple_of(chunk * span + core * own, own), own)
        other_rows = pl.ds(pl.multiple_of(chunk * span + (1 - core) * own, own), own)

        def send_near(which):
            spots = (which, chunk)
            return send(
                k.part.at[which, other_rows],
                k.near.at[spots],
                k.near_send.at[spots],
                k.near_recv.at[spots],
                {"tensor": partner},
                "near",
                0.2 * 4 / CHUNKS,
            )

        def send_far(which, copy):
            spots = (which, chunk)
            copy[0].wait_recv()
            both = k.near[spots].astype(wide) + k.part[which, own_rows].astype(wide)
            k.chip[spots] = both.astype(low)
            return send(
                k.chip.at[spots],
                k.far.at[spots],
                k.far_send.at[spots],
                k.far_recv.at[spots],
                {"tensor": across},
                "far",
                2.1 * 4 / CHUNKS,
            )

        def take_far(which, copy):
            copy[0].wait_recv()
            return k.chip[which, chunk].astype(wide) + k.far[which, chunk].astype(wide)

        def trade(which, ref):
            spots = (which, chunk)
            return send(
                ref.at[own_rows],
                ref.at[own_rows],
                k.ex_send.at[spots],
                k.ex_recv.at[spots],
                {"tensor": partner},
                "near",
                0.2 * 4 / CHUNKS,
            )

        yield ("mixed",), (), COST[0], None
        k.part[SUM_ATTN, all_rows] = dot_nt(k.mixed[all_rows], k.full[ATTN, :, 3 * group :]).astype(low)
        copy = send_near(SUM_ATTN)
        yield (), (copy,), COST[1], None
        copy = send_far(SUM_ATTN, copy)
        yield (), (copy,), COST[2], None
        attn = take_far(SUM_ATTN, copy)
        normed, inverse = normalize(k.tokens[own_rows].astype(wide) + attn + k.norm[0:1])
        k.normed1[chunk] = normed
        k.inverse1[chunk] = inverse
        hidden = normed * k.norm[1:2] + k.norm[2:3]
        k.hidden[chunk] = hidden
        k.hidden_low[own_rows] = hidden.astype(low)
        copy = trade(EX_HIDDEN, k.hidden_low)
        yield all_of(UP), (copy,), COST[3], None
        copy[0].wait_recv()
        pre = dot_nn(k.hidden_low[all_rows], k.full[UP]) + k.up_bias[...]
        below = 0.5 * (1.0 + lax.erf(pre * root_half))
        k.act[all_rows] = (pre * below).astype(low)
        k.slope[all_rows] = below + pre * jnp.exp(-0.5 * pre * pre) * normal_peak
        yield all_of(DOWN), (), COST[4], None
        k.part[SUM_FFN, all_rows] = dot_nt(k.act[all_rows], k.full[DOWN]).astype(low)
        copy = send_near(SUM_FFN)
        yield (), (copy,), COST[1], None
        copy = send_far(SUM_FFN, copy)
        yield (), (copy,), COST[5], None
        ffn = take_far(SUM_FFN, copy)
        normed, inverse = normalize(k.hidden[chunk] + ffn + k.norm[3:4])
        k.out[own_rows] = (normed * k.norm[4:5] + k.norm[5:6]).astype(low)
        out_copy = trade(EX_OUT, k.out)
        positions = lax.broadcasted_iota(jnp.int32, (own, 1), 0) + (chunk * span + core * own)
        dout = k.cot[own_rows].astype(wide) * (positions < length).astype(wide)
        dres2 = norm_back(dout, normed, inverse, k.norm[4:5])
        k.dres2[chunk] = dres2
        k.dres2_low[own_rows] = dres2.astype(low)
        two_copy = trade(EX_TWO, k.dres2_low)
        k.norm_acc[chunk, 3:4] = column_sum(dres2)
        k.norm_acc[chunk, 4:5] = column_sum(dout * normed)
        k.norm_acc[chunk, 5:6] = column_sum(dout)
        k.norm_acc[chunk, 6:8] = jnp.zeros((2, width), wide)
        yield (), (two_copy, out_copy), 0.02, None
        two_copy[0].wait_recv()
        out_copy[0].wait_recv()
        stores.append(pltpu.make_async_copy(k.out.at[all_rows], k.out_hbm.at[all_rows], k.store_sem.at[0, chunk]))
        stores[-1].start()
        done.add(("two", chunk))
        yield (), (), COST[6], None
        dpre = dot_nn(k.dres2_low[all_rows], k.full[DOWN]) * k.slope[all_rows]
        k.bias_acc[chunk] = column_sum(dpre)
        k.dpre_low[all_rows] = dpre.astype(low)
        k.part[SUM_BACK, all_rows] = dot_nt(k.dpre_low[all_rows], k.full[UP]).astype(low)
        done.add(("dpre", chunk))
        copy = send_near(SUM_BACK)
        yield (), (copy,), COST[1], None
        copy = send_far(SUM_BACK, copy)
        yield (), (copy,), COST[7], None
        dhidden = k.dres2[chunk] + take_far(SUM_BACK, copy)
        normed = k.normed1[chunk]
        dres1 = norm_back(dhidden, normed, k.inverse1[chunk], k.norm[1:2])
        k.dres1[chunk] = dres1
        k.dres1_low[own_rows] = dres1.astype(low)
        copy = trade(EX_ONE, k.dres1_low)
        k.norm_acc[chunk, 0:1] = column_sum(dres1)
        k.norm_acc[chunk, 1:2] = column_sum(dhidden * normed)
        k.norm_acc[chunk, 2:3] = column_sum(dhidden)
        done.add(("sums", chunk))
        yield (), (copy,), COST[8], None
        copy[0].wait_recv()
        done.add(("one", chunk))
        dmix = dot_nn(k.dres1_low[all_rows], k.full[ATTN, :, 3 * group :]).astype(low)
        for head in range(HEADS_HERE):
            k.dmix[head, all_rows] = dmix[:, head * HDIM : (head + 1) * HDIM]
        done.add(("dmix", chunk))
        yield ("dqkv",), (), COST[9], None
        k.part[SUM_INPUT, all_rows] = dot_nt(k.dqkv[all_rows], k.full[ATTN]).astype(low)
        copy = send_near(SUM_INPUT)
        yield (), (copy,), COST[1], None
        copy = send_far(SUM_INPUT, copy)
        yield (), (copy,), COST[10], None
        total = k.dres1[chunk] + take_far(SUM_INPUT, copy)
        k.gin[own_rows] = total.astype(low)
        copy = trade(EX_INPUT, k.gin)
        yield (), (copy,), 0.02, None
        copy[0].wait_recv()
        stores.append(pltpu.make_async_copy(k.gin.at[all_rows], k.gin_hbm.at[all_rows], k.store_sem.at[1, chunk]))
        stores[-1].start()

    def turn(left, right, index, columns):
        k.turned[...] = left[...].T
        grad_tile(index, k.turned, right, columns)

    def grad_tile(index, left_t, right, columns):
        def body(step, carry):
            spot = pl.ds(pl.multiple_of(step * 256, 256), 256)
            product = dot_nn(left_t[spot], right[...]).astype(low)
            k.grads[index, spot, columns] = product[:, : columns.size]
            return carry

        lax.fori_loop(0, width // 256, body, 0)

    def grad_down():
        yield every("two"), (), 1.2, None
        turn(k.dres2_low, k.act, DOWN, pl.ds(0, width))
        done.add(("grad", DOWN))

    def grad_up():
        yield every("dpre"), (), 1.2, None
        turn(k.hidden_low, k.dpre_low, UP, pl.ds(0, width))
        done.add(("grad", UP))

    def grad_attn():
        yield every("one"), (), 0.5, None
        turn(k.dres1_low, k.mixed, ATTN, pl.ds(3 * group, group))
        yield ("dqkv",), (), 1.0, None
        grad_tile(ATTN, k.tokens_t, k.dqkv, pl.ds(0, 3 * group))
        done.add(("grad", ATTN))

    def attention_back():
        for head in range(HEADS_HERE):
            yield every("dmix"), (), 1.4, None
            start = head * HDIM
            dkey, dvalue = 0.0, 0.0
            for step in range(rows // 256):
                spot = pl.ds(step * 256, 256)
                dprob = dot_nt(k.value[head], k.dmix[head, spot])
                probs = k.probs[head, :, spot]
                total = jnp.sum(probs * dprob, 0, keepdims=True)
                dscore = (probs * (dprob - total)).astype(low)
                k.dquery_t[start : start + HDIM, spot] = dot_nn(k.key_t[head], dscore)
                dkey += dot_nn(dscore, k.query[head, spot])
                dvalue += dot_nn(probs.astype(low), k.dmix[head, spot])
            k.dqkv[:, group + start : group + start + HDIM] = dkey.astype(low)
            k.dqkv[:, 2 * group + start : 2 * group + start + HDIM] = dvalue.astype(low)
            k.small[1:2, 384 + start : 384 + start + HDIM] = column_sum(dvalue)
        yield (), (), 0.3, None
        dquery = k.dquery_t[...].T
        k.dqkv[:, :group] = dquery.astype(low)
        k.small[0:1, 384 : 384 + group] = column_sum(dquery)
        done.add("dqkv")

    def small_sums():
        yield every("sums"), (), 0.1, None
        norm_total = k.norm_acc[0]
        bias_total = k.bias_acc[0]
        for chunk in range(1, CHUNKS):
            norm_total += k.norm_acc[chunk]
            bias_total += k.bias_acc[chunk]
        half_width = width // 2
        k.norm_half[0] = norm_total[:, :half_width]
        k.norm_half[1] = norm_total[:, half_width:]
        pair = send(
            k.norm_half.at[1 - core],
            k.norm_in,
            k.pair_send.at[0],
            k.pair_recv.at[0],
            {"tensor": partner},
            "near",
            0.05,
        )
        for spot in range(4):
            k.small[2 + spot : 3 + spot, 384 : 384 + group] = bias_total[:, spot * group : (spot + 1) * group]
        yield ("dqkv",), (pair,), 0.2, None
        pair[0].wait_recv()
        k.small[:, :half_width] = k.norm_half[core] + k.norm_in[...]
        shared = [
            send(
                k.small,
                k.slots.at[me],
                k.dp_send.at[shift - 1],
                k.dp_recv.at[shift - 1],
                {"dp": (me + shift) % RING},
                shift % 2,
                0.5,
            )
            for shift in range(1, RING)
        ]
        k.slots[me] = k.small[...]
        yield (), tuple(shared), 0.2, None
        for copy in shared:
            copy[0].wait_recv()
        small_total = k.slots[0]
        for index in range(1, RING):
            small_total += k.slots[index]
        k.bias_out[...] = small_total[:, 384:640]
        k.norm_fin[core] = small_total[:, :half_width]
        pair = send(
            k.norm_fin.at[core],
            k.norm_fin.at[core],
            k.pair_send.at[1],
            k.pair_recv.at[1],
            {"tensor": partner},
            "near",
            0.05,
        )
        yield (), (pair,), 0.05, None
        pair[0].wait_recv()
        k.norm_out[...] = k.norm_fin[...]

    plans = [((3, 0), prepare()), ((2, 0), attention())]
    for index in range(3):
        for half in range(2):
            for way in range(2):
                plans.append(((0, index, half), gather_chain(index, half, way)))
                plans.append(((0, 2 - index, half), scatter_chain(index, half, way)))
    plans += [((2, 1 + chunk), chunk_steps(chunk)) for chunk in range(CHUNKS)]
    plans += [((1, 0), grad_down()), ((2, 9), attention_back()), ((3, 1), grad_up()), ((1, 1), grad_attn())]
    plans.append(((5, 0), small_sums()))
    for index, total in ((DOWN, k.tot2), (UP, k.tot1), (ATTN, k.tot0)):
        for half in range(2):
            plans.append(((4, half), scatter_end(index, half, total)))
    run_all(plans)
    for copy in sent:
        copy.wait_send()
    for store in stores:
        store.wait()


def run_layer(tokens, cotangent, lengths, in_weight, out_weight, in_bias, norm_vec):
    rows, width = tokens.shape
    slab, group = in_weight.shape[1:]
    scratch = scratch_list(rows, width, slab, group)
    names = INPUTS + OUTPUTS + tuple(scratch)
    anywhere = pl.BlockSpec(memory_space=pl.ANY)
    inside = pl.BlockSpec(memory_space=pltpu.VMEM)
    scalar = pl.BlockSpec(memory_space=pltpu.SMEM)
    total = jax.ShapeDtypeStruct((slab, width), jnp.float32)
    like = jax.ShapeDtypeStruct((rows, width), jnp.bfloat16)
    return pl.pallas_call(
        functools.partial(layer_kernel, names),
        out_shape=(
            like,
            like,
            total,
            total,
            total,
            jax.ShapeDtypeStruct((2, 8, width // 2), jnp.float32),
            jax.ShapeDtypeStruct((8, 256), jnp.float32),
        ),
        in_specs=[anywhere, anywhere, scalar] + [anywhere] * 4,
        out_specs=(anywhere,) * 2 + (inside,) * (len(OUTPUTS) - 2),
        scratch_shapes=list(scratch.values()),
        compiler_params=pltpu.CompilerParams(
            collective_id=0, has_side_effects=True, vmem_limit_bytes=56 * 2**20
        ),
        name="layer",
    )(tokens, cotangent, lengths, in_weight, out_weight, in_bias, norm_vec)


def scatter_plain(grads):
    share = lax.psum_scatter(grads, "dp", scatter_dimension=0, tiled=True)
    return share.astype(jnp.float32)


def matmul(left_op, right_op):
    return jnp.dot(left_op, right_op, preferred_element_type=jnp.float32)


def inner_rows(left_op, right_op):
    return lax.dot_general(
        left_op, right_op, (((0,), (0,)), ((), ())), preferred_element_type=jnp.float32
    )


def times_transposed(left_op, right_op):
    return lax.dot_general(
        left_op, right_op, (((1,), (1,)), ((), ())), preferred_element_type=jnp.float32
    )


def layer_norm(summed_rows, gain_vec, shift_vec):
    center = jnp.mean(summed_rows, -1, keepdims=True)
    offset = summed_rows - center
    inverse = lax.rsqrt(jnp.mean(offset * offset, -1, keepdims=True) + norm_eps)
    normed = offset * inverse
    return (normed * gain_vec + shift_vec, normed, inverse)


def norm_back(upstream, normed, inverse, gain_vec):
    scaled = upstream * gain_vec
    return inverse * (
        scaled
        - jnp.mean(scaled, -1, keepdims=True)
        - normed * jnp.mean(scaled * normed, -1, keepdims=True)
    )


def gelu_value(pre_act):
    return 0.5 * pre_act * (1.0 + jax.scipy.special.erf(pre_act * root_half))


def gelu_slope(pre_act):
    return (
        0.5 * (1.0 + jax.scipy.special.erf(pre_act * root_half))
        + pre_act * jnp.exp(-0.5 * pre_act * pre_act) * normal_peak
    )


def score_block(query_heads, key_heads, length):
    seq_len = query_heads.shape[0]
    scale_factor = query_heads.shape[-1] ** (-0.5)
    scores = (
        jnp.einsum("qhe,khe->hqk", query_heads, key_heads, preferred_element_type=jnp.float32)
        * scale_factor
    )
    usable = lax.broadcasted_iota(jnp.int32, (1, 1, seq_len), 2) < length
    return jnp.where(usable, scores, masked_score)


def attend_forward(operands):
    query_heads, key_heads, value_heads, length = operands
    scores = score_block(query_heads, key_heads, length)
    highest = jnp.max(scores, -1, keepdims=True)
    log_total = highest + jnp.log(jnp.sum(jnp.exp(scores - highest), -1, keepdims=True))
    probs_low = jnp.exp(scores - log_total).astype(jnp.bfloat16)
    mixed_heads = jnp.einsum(
        "hqk,khe->qhe", probs_low, value_heads, preferred_element_type=jnp.float32
    )
    return (mixed_heads.astype(jnp.bfloat16), log_total)


def attend_backward(operands):
    query_heads, key_heads, value_heads, grad_heads, log_total, length = operands
    scale_factor = query_heads.shape[-1] ** (-0.5)
    scores = score_block(query_heads, key_heads, length)
    probs = jnp.exp(scores - log_total)
    probs_low = probs.astype(jnp.bfloat16)
    grad_probs = jnp.einsum(
        "qhe,khe->hqk", grad_heads, value_heads, preferred_element_type=jnp.float32
    )
    row_dot = jnp.sum(probs * grad_probs, -1, keepdims=True)
    grad_scores = (probs * (grad_probs - row_dot) * scale_factor).astype(jnp.bfloat16)
    grad_query = jnp.einsum(
        "hqk,khe->qhe", grad_scores, key_heads, preferred_element_type=jnp.float32
    )
    grad_keys = jnp.einsum(
        "hqk,qhe->khe", grad_scores, query_heads, preferred_element_type=jnp.float32
    )
    grad_values = jnp.einsum(
        "hqk,qhe->khe", probs_low, grad_heads, preferred_element_type=jnp.float32
    )
    return (grad_query, grad_keys, grad_values)


def adam_update(param, grad, moments, decay):
    first = beta_first * moments[0] + (1.0 - beta_first) * grad
    second = beta_second * moments[1] + (1.0 - beta_second) * grad * grad
    first_hat = first / (1.0 - beta_first**step_count)
    second_hat = second / (1.0 - beta_second**step_count)
    new_param = param - learn_rate * (first_hat / (jnp.sqrt(second_hat) + adam_eps) + decay * param)
    return (new_param, jnp.stack([first, second]))


def adam_store(param, grad, moments, decay, new_param, new_moments):
    first = beta_first * moments[0] + (1.0 - beta_first) * grad
    second = beta_second * moments[1] + (1.0 - beta_second) * grad * grad
    first_hat = first / (1.0 - beta_first**step_count)
    second_hat = second / (1.0 - beta_second**step_count)
    step = first_hat / (jnp.sqrt(second_hat) + adam_eps) + decay * param
    new_param[...] = param - learn_rate * step
    new_moments[0][...] = first
    new_moments[1][...] = second


def adam_kernel(*refs):
    tot0, tot1, tot2, norm_ref, bias_ref, out_from, gin_from = refs[:7]
    params, moments = refs[7:11], refs[11:15]
    out_to, gin_to = refs[15:17]
    grads, new_params, new_moments = refs[17:21], refs[21:25], refs[25:29]
    held = (refs[29:33], refs[33:37])
    fresh = (refs[37:40], refs[40:43])
    pass_ref, pass_sem, in_sem, out_sem = refs[43:]
    width = params[0].shape[2]
    order = list(range(8, 12)) + list(range(4, 8)) + list(range(4))

    def place_of(index):
        if index == 3 or index >= 8:
            return 1, 0 if index == 3 else index - 7
        return 0, index if index < 3 else index - 1

    loads = {}
    for index in order:
        group, spot = place_of(index)
        loads[index] = [
            pltpu.make_async_copy(params[group].at[spot], held[group][0].at[spot], in_sem.at[index, 0]),
            pltpu.make_async_copy(moments[group].at[0, spot], held[group][1].at[spot], in_sem.at[index, 1]),
            pltpu.make_async_copy(moments[group].at[1, spot], held[group][2].at[spot], in_sem.at[index, 2]),
        ]
        for copy in loads[index]:
            copy.start()
    passing = [
        pltpu.make_async_copy(source, pass_ref.at[spot], pass_sem.at[0, spot])
        for spot, source in enumerate((out_from, gin_from))
    ]
    for copy in passing:
        copy.start()
    stores = []
    for index in order:
        if index == 4:
            for spot, target in enumerate((out_to, gin_to)):
                passing[spot].wait()
                stores.append(pltpu.make_async_copy(pass_ref.at[spot], target, pass_sem.at[1, spot]))
                stores[-1].start()
        group, spot = place_of(index)
        source, place = (tot0, tot1, tot2)[index // 4], index % 4
        grad = source[:, place * width : (place + 1) * width]
        if group:
            grad = grad.T
        for copy in loads[index]:
            copy.wait()
        held[group][3][spot] = grad
        adam_store(
            held[group][0][spot],
            grad,
            (held[group][1][spot], held[group][2][spot]),
            weight_decay,
            fresh[group][0].at[spot],
            (fresh[group][1].at[spot], fresh[group][2].at[spot]),
        )
        results = (
            (held[group][3].at[spot], grads[group].at[spot]),
            (fresh[group][0].at[spot], new_params[group].at[spot]),
            (fresh[group][1].at[spot], new_moments[group].at[0, spot]),
            (fresh[group][2].at[spot], new_moments[group].at[1, spot]),
        )
        for turn, (source, target) in enumerate(results):
            copy = pltpu.make_async_copy(source, target, out_sem.at[index, turn])
            copy.start()
            stores.append(copy)
    norm_grad = jnp.concatenate([norm_ref[0, :6], norm_ref[1, :6]], 1)
    for group, grad in ((2, bias_ref[:6, :width]), (3, norm_grad)):
        grads[group][...] = grad
        adam_store(
            params[group][...],
            grad,
            (moments[group][:, 0, :], moments[group][:, 1, :]),
            0.0,
            new_params[group],
            (new_moments[group].at[:, 0, :], new_moments[group].at[:, 1, :]),
        )
    for copy in stores:
        copy.wait()


def update_here(rows, totals, params, moments):
    moments = moments[:2] + tuple(m.swapaxes(0, 1) for m in moments[2:])
    inside = pl.BlockSpec(memory_space=pltpu.VMEM)
    anywhere = pl.BlockSpec(memory_space=pl.ANY)
    kinds = [anywhere, anywhere, inside, inside]
    shapes = [jax.ShapeDtypeStruct(a.shape, jnp.float32) for a in params + params + moments]
    blocks = [pltpu.VMEM(params[group].shape, jnp.float32) for group in (0,) * 4 + (1,) * 4]
    blocks += [pltpu.VMEM(params[group].shape, jnp.float32) for group in (0,) * 3 + (1,) * 3]
    dma = pltpu.SemaphoreType.DMA
    results = pl.pallas_call(
        adam_kernel,
        out_shape=tuple(jax.ShapeDtypeStruct(a.shape, a.dtype) for a in rows) + tuple(shapes),
        in_specs=[inside] * len(totals) + [anywhere] * 2 + kinds * 2,
        out_specs=tuple([anywhere] * 2 + kinds * 3),
        scratch_shapes=blocks + [pltpu.VMEM((2,) + rows[0].shape, rows[0].dtype), dma((2, 2)), dma((12, 3)), dma((12, 4))],
        name="adam",
    )(*totals, *rows, *params, *moments)
    return results[:-2] + tuple(m.swapaxes(0, 1) for m in results[-2:])


def update_plain(share, rest, small, params, moments):
    group_width, width = params[0].shape[2], params[3].shape[1]
    total = jnp.concatenate([share, rest], 1)
    blocks = [total[:, k * group_width : (k + 1) * group_width] for k in range(12)]
    grads = (
        jnp.stack(blocks[:3] + blocks[4:8]),
        jnp.stack([blocks[3]] + blocks[8:]).swapaxes(1, 2),
        small[:6, width : width + group_width],
        small[:6, :width],
    )
    decays = (weight_decay, weight_decay, 0.0, 0.0)
    news = [adam_update(*group) for group in zip(params, grads, moments, decays)]
    return grads + tuple(n[0] for n in news) + tuple(n[1] for n in news)


def plain_layer(
    tokens,
    cotangent,
    lengths,
    in_weight,
    out_weight,
    in_bias,
    norm_vec,
    in_moments,
    out_moments,
    bias_moments,
    norm_moments,
):
    seq_count, seq_len, width = tokens.shape
    row_count = seq_count * seq_len
    in_low = in_weight.astype(jnp.bfloat16)
    out_low = out_weight.astype(jnp.bfloat16).swapaxes(1, 2)
    share = jnp.concatenate(list(in_low[:3]) + [out_low[0]], 1)
    rest = jnp.concatenate(list(in_low[3:]) + list(out_low[1:]), 1)
    first_full = lax.all_gather(share, "dp", axis=0, tiled=True)
    second_full = lax.all_gather(rest, "dp", axis=0, tiled=True)
    group_width = in_weight.shape[2]
    heads_here = group_width // HDIM
    w_qkv = first_full[:, : 3 * group_width]
    w_proj = first_full[:, 3 * group_width :]
    bias_up = in_bias[2:6].reshape(1, 4 * group_width)

    def split_heads(flat_rows):
        return flat_rows.reshape(seq_count, seq_len, heads_here, HDIM)

    flat_tokens = tokens.reshape(row_count, width)
    qkv = matmul(flat_tokens, w_qkv)
    query = (qkv[:, :group_width] + in_bias[0]).astype(jnp.bfloat16)
    keys_low = qkv[:, group_width : 2 * group_width].astype(jnp.bfloat16)
    values_low = (qkv[:, 2 * group_width :] + in_bias[1]).astype(jnp.bfloat16)
    mixed_heads, log_total = lax.map(
        attend_forward,
        (split_heads(query), split_heads(keys_low), split_heads(values_low), lengths),
    )
    mixed_flat = mixed_heads.reshape(row_count, group_width)
    attn_part = times_transposed(mixed_flat, w_proj).astype(jnp.bfloat16)
    attn_out = lax.psum(attn_part, "tensor")
    w_up = second_full[:, : 4 * group_width]
    w_down = second_full[:, 4 * group_width :]
    hidden, normed_one, inverse_one = layer_norm(
        flat_tokens.astype(jnp.float32) + attn_out.astype(jnp.float32) + norm_vec[0], norm_vec[1], norm_vec[2]
    )
    hidden_low = hidden.astype(jnp.bfloat16)
    pre_act = matmul(hidden_low, w_up) + bias_up
    act_low = gelu_value(pre_act).astype(jnp.bfloat16)
    ffn_part = times_transposed(act_low, w_down).astype(jnp.bfloat16)
    ffn_out = lax.psum(ffn_part, "tensor").astype(jnp.float32)
    out_rows, normed_two, inverse_two = layer_norm(
        hidden + ffn_out + norm_vec[3], norm_vec[4], norm_vec[5]
    )
    positions = lax.broadcasted_iota(jnp.int32, (seq_count, seq_len), 1)
    live_rows = (positions < lengths[:, None]).astype(jnp.float32).reshape(row_count, 1)
    grad_out = cotangent.reshape(row_count, width).astype(jnp.float32) * live_rows
    grad_two = norm_back(grad_out, normed_two, inverse_two, norm_vec[4])
    grad_two_low = grad_two.astype(jnp.bfloat16)
    grad_down = inner_rows(grad_two_low, act_low).astype(jnp.bfloat16)
    grad_act = matmul(grad_two_low, w_down)
    grad_pre = grad_act * gelu_slope(pre_act)
    grad_pre_low = grad_pre.astype(jnp.bfloat16)
    grad_up = inner_rows(hidden_low, grad_pre_low).astype(jnp.bfloat16)
    rest_grads = jnp.concatenate([grad_up, grad_down], 1)
    back_part = times_transposed(grad_pre_low, w_up).astype(jnp.bfloat16)
    back_sum = lax.psum(back_part, "tensor")
    grad_hidden = grad_two + back_sum.astype(jnp.float32)
    grad_one = norm_back(grad_hidden, normed_one, inverse_one, norm_vec[1])
    grad_one_low = grad_one.astype(jnp.bfloat16)
    grad_proj = inner_rows(grad_one_low, mixed_flat).astype(jnp.bfloat16)
    grad_mixed = matmul(grad_one_low, w_proj).astype(jnp.bfloat16)
    grad_query, grad_keys, grad_values = lax.map(
        attend_backward,
        (
            split_heads(query),
            split_heads(keys_low),
            split_heads(values_low),
            split_heads(grad_mixed),
            log_total,
            lengths,
        ),
    )
    grad_query = grad_query.reshape(row_count, group_width)
    grad_keys = grad_keys.reshape(row_count, group_width)
    grad_values = grad_values.reshape(row_count, group_width)
    qkv_grad_low = jnp.concatenate([grad_query, grad_keys, grad_values], 1).astype(jnp.bfloat16)
    input_part = times_transposed(qkv_grad_low, w_qkv).astype(jnp.bfloat16)
    grad_qkv = inner_rows(flat_tokens, qkv_grad_low).astype(jnp.bfloat16)
    first_grads = jnp.concatenate([grad_qkv, grad_proj], 1)
    bias_rows = jnp.concatenate(
        [jnp.sum(grad_query, 0), jnp.sum(grad_values, 0), jnp.sum(grad_pre, 0)]
    ).reshape(6, group_width)
    norm_rows = jnp.stack(
        [
            jnp.sum(grad_one, 0),
            jnp.sum(grad_hidden * normed_one, 0),
            jnp.sum(grad_hidden, 0),
            jnp.sum(grad_two, 0),
            jnp.sum(grad_out * normed_two, 0),
            jnp.sum(grad_out, 0),
        ]
    )
    small = jnp.pad(jnp.concatenate([norm_rows, bias_rows], 1), ((0, 2), (0, 64)))
    share_total = scatter_plain(first_grads)
    rest_total = scatter_plain(rest_grads)
    input_sum = lax.psum(input_part, "tensor")
    small_total = lax.psum(small, "dp")
    grad_input = grad_one + input_sum.astype(jnp.float32)
    params = (in_weight, out_weight, in_bias, norm_vec)
    moments = (in_moments, out_moments, bias_moments, norm_moments)
    updates = update_plain(share_total, rest_total, small_total, params, moments)
    output = out_rows.astype(jnp.bfloat16).reshape(seq_count, seq_len, width)
    grad_tokens = grad_input.astype(jnp.bfloat16).reshape(seq_count, seq_len, width)
    return (
        output,
        grad_tokens,
    ) + tuple(updates)


def local(*operands):
    tokens, cotangent, lengths, in_weight, out_weight, in_bias, norm_vec = operands[:7]
    ring = lax.axis_size("dp") == RING and lax.axis_size("tensor") == 4
    if not ring or tokens.shape[0] != 1:
        return plain_layer(*operands)
    out, grad_tokens, *totals = run_layer(
        tokens[0], cotangent[0], lengths, in_weight, out_weight, in_bias, norm_vec
    )
    results = update_here((out, grad_tokens), tuple(totals), operands[3:7], operands[7:])
    return (results[0][None], results[1][None]) + tuple(results[2:])


def solution(mesh):
    in_specs = (
        P("dp", None, None),
        P("dp", None, None),
        P("dp"),
        P(None, "dp", "tensor"),
        P(None, "tensor", "dp"),
        P(None, "tensor"),
        P(),
        P(None, None, "dp", "tensor"),
        P(None, None, "tensor", "dp"),
        P(None, None, "tensor"),
        P(),
    )
    out_specs = (
        P("dp", None, None),
        P("dp", None, None),
        P(None, "dp", "tensor"),
        P(None, "tensor", "dp"),
        P(None, "tensor"),
        P(),
        P(None, "dp", "tensor"),
        P(None, "tensor", "dp"),
        P(None, "tensor"),
        P(),
        P(None, None, "dp", "tensor"),
        P(None, None, "tensor", "dp"),
        P(None, None, "tensor"),
        P(),
    )
    return jax.shard_map(local, mesh=mesh, in_specs=in_specs, out_specs=out_specs, check_vma=False)
```

```python
import functools

import jax
import jax.numpy as jnp
from jax import lax
from jax.experimental import pallas as pl
from jax.experimental.pallas import tpu as pltpu
from jax.sharding import PartitionSpec as P

HDIM = 64


norm_eps = 1e-12
masked_score = -1e30
learn_rate = 0.005
beta_first = 0.9
beta_second = 0.999
adam_eps = 1e-08
weight_decay = 0.01
step_count = 2.0
root_half = 0.7071067811865476
normal_peak = 0.3989422804014327


RING = 8
CHUNKS = 2
PIECES = 3
PIECE_TIME = 3.2 / PIECES
LINK_DELAY = {"near": 1.5, "far": 2.2, 0: 2.0, 1: 2.0}
FILL_LIMIT = (0.3, 2.0, 3.0)
WAIT_TIME = 0.06
SCATTER_LIMIT = 99.0
COST = [c * 3.6 / CHUNKS for c in (0.2, 0.1, 0.25, 0.6, 0.3, 0.45, 0.6, 0.35, 0.2, 0.3, 0.15)]
HEADS_HERE = 3
MESH = pl.DeviceIdType.MESH
ATTN, UP, DOWN = 0, 1, 2
SUM_ATTN, SUM_FFN, SUM_BACK, SUM_INPUT = 0, 1, 2, 3
EX_HIDDEN, EX_OUT, EX_TWO, EX_ONE, EX_INPUT = 0, 1, 2, 3, 4


def ring_place(index):
    depth, side = index // 2, index % 2
    return depth + side * (RING - 1 - 2 * depth)


def ring_device(place):
    side = place // (RING // 2)
    depth = place + side * (RING - 1 - 2 * place)
    return 2 * depth + side


def dot_nn(left_op, right_op):
    return jnp.dot(left_op, right_op, preferred_element_type=jnp.float32)


def dot_nt(left_op, right_op):
    return lax.dot_general(
        left_op, right_op, (((1,), (1,)), ((), ())), preferred_element_type=jnp.float32
    )


def normalize(rows):
    center = jnp.mean(rows, -1, keepdims=True)
    offset = rows - center
    inverse = lax.rsqrt(jnp.mean(offset * offset, -1, keepdims=True) + norm_eps)
    return offset * inverse, inverse


def hops(index, half, way):
    return 3 + (half + way + 1 + index) % 2


def column_sum(rows):
    return jnp.sum(rows, 0, keepdims=True)


INPUTS = ("tokens_hbm", "cot_hbm", "lengths", "inw_hbm", "outw_hbm", "bias_hbm", "norm_hbm")
OUTPUTS = ("out_hbm", "gin_hbm", "tot0", "tot1", "tot2", "norm_out", "bias_out")


def scratch_list(rows, width, slab, group):
    own = rows // (2 * CHUNKS)
    piece = slab // PIECES
    low, wide = jnp.bfloat16, jnp.float32
    dma = pltpu.SemaphoreType.DMA
    vmem = pltpu.VMEM
    heads = (HEADS_HERE, rows, HDIM)
    turned = (HEADS_HERE, HDIM, rows)
    return {
        "tokens": vmem((rows, width), low),
        "out": vmem((rows, width), low),
        "gin": vmem((rows, width), low),
        "store_sem": dma((2, CHUNKS)),
        "cot": vmem((rows, width), low),
        "inw": vmem((7, slab, group), wide),
        "outw": vmem((5, group, slab), wide),
        "bias": vmem((6, group), wide),
        "norm": vmem((6, width), wide),
        "full": vmem((3, width, width), low),
        "grads": vmem((3, width, width), low),
        "arrived": vmem((3, 4, PIECES, 2, piece, width), low),
        "leaving": vmem((3, 4, PIECES, 2, piece, width), low),
        "tokens_t": vmem((width, rows), low),
        "qkv_bias": vmem((1, width), wide),
        "up_bias": vmem((1, width), wide),
        "query": vmem(heads, low),
        "key": vmem(heads, low),
        "value": vmem(heads, low),
        "dmix": vmem(heads, low),
        "key_t": vmem(turned, low),
        "value_t": vmem(turned, low),
        "probs": vmem((HEADS_HERE, rows, rows), wide),
        "mixed_t": vmem((group, rows), low),
        "mixed": vmem((rows, group), low),
        "dquery_t": vmem((group, rows), wide),
        "dqkv": vmem((rows, width), low),
        "part": vmem((4, rows, width), low),
        "near": vmem((4, CHUNKS, own, width), low),
        "chip": vmem((4, CHUNKS, own, width), low),
        "far": vmem((4, CHUNKS, own, width), low),
        "hidden": vmem((CHUNKS, own, width), wide),
        "normed1": vmem((CHUNKS, own, width), wide),
        "inverse1": vmem((CHUNKS, own, 1), wide),
        "dres2": vmem((CHUNKS, own, width), wide),
        "dres1": vmem((CHUNKS, own, width), wide),
        "hidden_low": vmem((rows, width), low),
        "dres2_low": vmem((rows, width), low),
        "dres1_low": vmem((rows, width), low),
        "act": vmem((rows, width), low),
        "slope": vmem((rows, width), wide),
        "dpre_low": vmem((rows, width), low),
        "norm_acc": vmem((CHUNKS, 8, width), wide),
        "bias_acc": vmem((CHUNKS, 1, width), wide),
        "norm_half": vmem((2, 8, width // 2), wide),
        "norm_in": vmem((8, width // 2), wide),
        "small": vmem((8, 640), wide),
        "norm_fin": vmem((2, 8, width // 2), wide),
        "turned": vmem((width, rows), low),
        "slots": vmem((RING, 8, 640), wide),
        "load_sem": dma((8,)),
        "g_send": dma((3, 4, PIECES, 2)),
        "g_recv": dma((3, 4, PIECES, 2)),
        "s_send": dma((3, 4, PIECES, 2)),
        "s_recv": dma((3, 4, PIECES, 2)),
        "near_send": dma((4, CHUNKS)),
        "near_recv": dma((4, CHUNKS)),
        "far_send": dma((4, CHUNKS)),
        "far_recv": dma((4, CHUNKS)),
        "ex_send": dma((5, CHUNKS)),
        "ex_recv": dma((5, CHUNKS)),
        "dp_send": dma((RING - 1,)),
        "dp_recv": dma((RING - 1,)),
        "pair_send": dma((2,)),
        "pair_recv": dma((2,)),
    }


class Names:
    pass


def layer_kernel(names, *refs):
    k = Names()
    for name, ref in zip(names, refs):
        setattr(k, name, ref)
    rows, width = k.tokens.shape
    group, slab = k.bias.shape[1], k.inw.shape[1]
    span = rows // CHUNKS
    own = span // 2
    piece = slab // PIECES
    low, wide = jnp.bfloat16, jnp.float32
    me, tensor = lax.axis_index("dp"), lax.axis_index("tensor")
    core = tensor % 2
    partner, across = tensor + 1 - 2 * core, (tensor + 2) % 4
    place = ring_place(me)
    targets = (ring_device((place + 1) % RING), ring_device((place + RING - 1) % RING))
    passed, stores, sent, done, free = [], [], [], set(), dict.fromkeys(("near", "far", 0, 1), 0.0)
    clock = [0.0]

    def send(source, target, send_sem, recv_sem, device, link, busy):
        copy = pltpu.make_async_remote_copy(
            src_ref=source,
            dst_ref=target,
            send_sem=send_sem,
            recv_sem=recv_sem,
            device_id=device,
            device_id_type=MESH,
        )
        copy.start()
        free[link] = max(free[link], clock[0]) + busy
        sent.append((free[link] + LINK_DELAY[link], len(sent), copy))
        return copy, free[link] + LINK_DELAY[link]

    def run_all(plans):
        active = [[rank, plan, next(plan)] for rank, plan in plans]
        while active:
            best = None
            for item in active:
                rank, plan, (flags, flights, cost, gate) = item
                if any(flag not in done for flag in flags):
                    continue
                ready = max([clock[0]] + [flight[1] for flight in flights])
                if gate:
                    limit = gate[1] if gate[2] else FILL_LIMIT[min(len(passed) // (2 * PIECES), 2)]
                    ready = max(ready, free[gate[0]] - limit)
                if best is None or (ready, rank) < best[0]:
                    best = (ready, rank), item
            (ready, rank), item = best
            turns = int((ready - clock[0]) / WAIT_TIME)
            for flight in sorted(sent)[:turns]:
                if flight[0] <= clock[0]:
                    flight[2].wait_send()
                    sent.remove(flight)
            clock[0] = ready + item[2][2]
            item[2] = next(item[1], None)
            if item[2] is None:
                active.remove(item)

    def slab_rows(owner, half):
        return pl.ds(pl.multiple_of(owner * slab + half * piece, piece), piece)

    def gather_chain(index, half, way):
        length = hops(index, half, way)
        flight = None
        for step in range(length):
            shift = RING - step if way == 0 else step
            spot = k.full.at[index, slab_rows(ring_device((place + shift) % RING), half)]
            spots = (index, step, half, way)
            gate = (way, 99.0, index == ATTN)
            if step:
                yield (), (flight,), 0.05, gate
                flight[0].wait_recv()
            else:
                yield (("own", index),), (), 0.05, gate
            flight = send(
                spot, spot, k.g_send.at[spots], k.g_recv.at[spots], {"dp": targets[way]}, way, PIECE_TIME
            )
        passed.append(index)
        yield (), (flight,), 0.02, None
        flight[0].wait_recv()
        done.add(("full", index, half, way))

    def all_of(index):
        return tuple(("full", index, half, way) for half in range(PIECES) for way in range(2))

    def every(name):
        return tuple((name, chunk) for chunk in range(CHUNKS))

    ends = {}

    def scatter_chain(index, half, way):
        length = hops(index, half, way)
        flight = None
        for step in range(length):
            shift = length - step if way == 0 else RING - length + step
            spot = (index, slab_rows(ring_device((place + shift) % RING), half))
            spots = (index, step, half, way)
            gate = (way, SCATTER_LIMIT, True)
            if step:
                yield (), (flight,), 0.08, gate
                flight[0].wait_recv()
                come = k.arrived[index, step - 1, half, way].astype(wide)
                k.leaving[spots] = (come + k.grads[spot].astype(wide)).astype(low)
                source = k.leaving.at[spots]
            else:
                yield (("grad", index),), (), 0.05, gate
                source = k.grads.at[spot]
            flight = send(
                source,
                k.arrived.at[spots],
                k.s_send.at[spots],
                k.s_recv.at[spots],
                {"dp": targets[way]},
                way,
                PIECE_TIME,
            )
        ends[index, half, way] = flight
        done.add(("end", index, half, way))

    def scatter_end(index, half, total):
        yield tuple(("end", index, half, way) for way in range(2)), (), 0.0, None
        yield (), tuple(ends[index, half, way] for way in range(2)), 0.1, None
        mine = k.grads[index, slab_rows(me, half)].astype(wide)
        for way in range(2):
            ends[index, half, way][0].wait_recv()
            mine += k.arrived[index, hops(index, half, way) - 1, half, way].astype(wide)
        total[half * piece : (half + 1) * piece] = mine

    loads = [
        pltpu.make_async_copy(source, target, k.load_sem.at[spot])
        for spot, (source, target) in enumerate(
            (
                (k.inw_hbm.at[:3], k.inw.at[:3]),
                (k.outw_hbm.at[:1], k.outw.at[:1]),
                (k.inw_hbm.at[3:], k.inw.at[3:]),
                (k.outw_hbm.at[1:], k.outw.at[1:]),
                (k.tokens_hbm, k.tokens),
                (k.bias_hbm, k.bias),
                (k.norm_hbm, k.norm),
                (k.cot_hbm, k.cot),
            )
        )
    ]
    for load in loads:
        load.start()
    barrier = pltpu.get_barrier_semaphore()
    greeted = [{"dp": (me + shift) % RING} for shift in range(1, RING)]
    greeted += [{"tensor": partner}, {"tensor": across}]
    for device in greeted:
        pl.semaphore_signal(barrier, inc=1, device_id=device, device_id_type=MESH)
    mine = pl.ds(pl.multiple_of(me * slab, slab), slab)

    def lower(index, first, blocks):
        for place_at, block in enumerate(blocks):
            start = (first + place_at) * group
            k.full[index, mine, start : start + group] = block.astype(low)
        done.add(("own", index))

    def prepare():
        yield (), (), 2.0, None
        loads[0].wait()
        loads[1].wait()
        lower(ATTN, 0, [k.inw[spot] for spot in range(3)] + [k.outw[0].T])
        pl.semaphore_wait(barrier, len(greeted))
        yield (), (), 0.4, None
        loads[2].wait()
        lower(UP, 0, [k.inw[3 + spot] for spot in range(4)])
        yield (), (), 0.6, None
        loads[3].wait()
        lower(DOWN, 0, [k.outw[1 + spot].T for spot in range(4)])
        yield (), (), 0.6, None
        for load in loads[4:]:
            load.wait()
        k.qkv_bias[...] = jnp.zeros_like(k.qkv_bias)
        k.qkv_bias[:, :group] = k.bias[0:1]
        k.qkv_bias[:, 2 * group : 3 * group] = k.bias[1:2]
        for spot in range(4):
            k.up_bias[:, spot * group : (spot + 1) * group] = k.bias[2 + spot : 3 + spot]
        k.dqkv[:, 3 * group :] = jnp.zeros((rows, width - 3 * group), low)
        k.small[...] = jnp.zeros_like(k.small)
        k.tokens_t[...] = k.tokens[...].T
        done.add("ready")

    def project(step, carry):
        spot = pl.ds(pl.multiple_of(step * 256, 256), 256)
        qkv = dot_nn(k.tokens[spot], k.full[ATTN]) + k.qkv_bias[...]
        for head in range(HEADS_HERE):
            start = head * HDIM
            k.query[head, spot] = (qkv[:, start : start + HDIM].astype(low) * HDIM**-0.5).astype(low)
            start += group
            k.key[head, spot] = qkv[:, start : start + HDIM].astype(low)
            start += group
            k.value[head, spot] = qkv[:, start : start + HDIM].astype(low)
        return carry

    length = k.lengths[0]

    def attention():
        yield all_of(ATTN) + ("ready",), (), 0.8, None
        lax.fori_loop(0, rows // 256, project, 0)
        yield (), (), 0.3, None
        usable = lax.broadcasted_iota(jnp.int32, (rows, 256), 0) < length
        for head in range(HEADS_HERE):
            k.value_t[head] = k.value[head].T
            k.key_t[head] = (k.key[head] * HDIM**-0.5).astype(low).T
        for head in range(HEADS_HERE):

            def attend(step, carry, head=head):
                spot = pl.ds(pl.multiple_of(step * 256, 256), 256)
                scores = jnp.where(usable, dot_nt(k.key[head], k.query[head, spot]), masked_score)
                highest = jnp.max(scores, 0, keepdims=True)
                raised = jnp.exp(scores - highest)
                probs = raised * (1.0 / jnp.sum(raised, 0, keepdims=True))
                k.probs[head, :, spot] = probs
                mixed = dot_nn(k.value_t[head], probs.astype(low))
                k.mixed_t[head * HDIM : (head + 1) * HDIM, spot] = mixed.astype(low)
                return carry

            yield (), (), 0.9, None
            lax.fori_loop(0, rows // 256, attend, 0)
        yield (), (), 0.15, None
        k.mixed[...] = k.mixed_t[...].T
        done.add("mixed")

    def chunk_steps(chunk):
        all_rows = pl.ds(chunk * span, span)
        own_rows = pl.ds(pl.multiple_of(chunk * span + core * own, own), own)
        other_rows = pl.ds(pl.multiple_of(chunk * span + (1 - core) * own, own), own)

        def send_near(which):
            spots = (which, chunk)
            return send(
                k.part.at[which, other_rows],
                k.near.at[spots],
                k.near_send.at[spots],
                k.near_recv.at[spots],
                {"tensor": partner},
                "near",
                0.2 * 4 / CHUNKS,
            )

        def send_far(which, copy):
            spots = (which, chunk)
            copy[0].wait_recv()
            both = k.near[spots].astype(wide) + k.part[which, own_rows].astype(wide)
            k.chip[spots] = both.astype(low)
            return send(
                k.chip.at[spots],
                k.far.at[spots],
                k.far_send.at[spots],
                k.far_recv.at[spots],
                {"tensor": across},
                "far",
                2.1 * 4 / CHUNKS,
            )

        def take_far(which, copy):
            copy[0].wait_recv()
            return k.chip[which, chunk].astype(wide) + k.far[which, chunk].astype(wide)

        def trade(which, ref):
            spots = (which, chunk)
            return send(
                ref.at[own_rows],
                ref.at[own_rows],
                k.ex_send.at[spots],
                k.ex_recv.at[spots],
                {"tensor": partner},
                "near",
                0.2 * 4 / CHUNKS,
            )

        yield ("mixed",), (), COST[0], None
        k.part[SUM_ATTN, all_rows] = dot_nt(k.mixed[all_rows], k.full[ATTN, :, 3 * group :]).astype(low)
        copy = send_near(SUM_ATTN)
        yield (), (copy,), COST[1], None
        copy = send_far(SUM_ATTN, copy)
        yield (), (copy,), COST[2], None
        attn = take_far(SUM_ATTN, copy)
        normed, inverse = normalize(k.tokens[own_rows].astype(wide) + attn + k.norm[0:1])
        k.normed1[chunk] = normed
        k.inverse1[chunk] = inverse
        hidden = normed * k.norm[1:2] + k.norm[2:3]
        k.hidden[chunk] = hidden
        k.hidden_low[own_rows] = hidden.astype(low)
        copy = trade(EX_HIDDEN, k.hidden_low)
        yield all_of(UP), (copy,), COST[3], None
        copy[0].wait_recv()
        pre = dot_nn(k.hidden_low[all_rows], k.full[UP]) + k.up_bias[...]
        below = 0.5 * (1.0 + lax.erf(pre * root_half))
        k.act[all_rows] = (pre * below).astype(low)
        k.slope[all_rows] = below + pre * jnp.exp(-0.5 * pre * pre) * normal_peak
        yield all_of(DOWN), (), COST[4], None
        k.part[SUM_FFN, all_rows] = dot_nt(k.act[all_rows], k.full[DOWN]).astype(low)
        copy = send_near(SUM_FFN)
        yield (), (copy,), COST[1], None
        copy = send_far(SUM_FFN, copy)
        yield (), (copy,), COST[5], None
        ffn = take_far(SUM_FFN, copy)
        normed, inverse = normalize(k.hidden[chunk] + ffn + k.norm[3:4])
        k.out[own_rows] = (normed * k.norm[4:5] + k.norm[5:6]).astype(low)
        out_copy = trade(EX_OUT, k.out)
        positions = lax.broadcasted_iota(jnp.int32, (own, 1), 0) + (chunk * span + core * own)
        dout = k.cot[own_rows].astype(wide) * (positions < length).astype(wide)
        dres2 = norm_back(dout, normed, inverse, k.norm[4:5])
        k.dres2[chunk] = dres2
        k.dres2_low[own_rows] = dres2.astype(low)
        two_copy = trade(EX_TWO, k.dres2_low)
        k.norm_acc[chunk, 3:4] = column_sum(dres2)
        k.norm_acc[chunk, 4:5] = column_sum(dout * normed)
        k.norm_acc[chunk, 5:6] = column_sum(dout)
        k.norm_acc[chunk, 6:8] = jnp.zeros((2, width), wide)
        yield (), (two_copy, out_copy), 0.02, None
        two_copy[0].wait_recv()
        out_copy[0].wait_recv()
        stores.append(pltpu.make_async_copy(k.out.at[all_rows], k.out_hbm.at[all_rows], k.store_sem.at[0, chunk]))
        stores[-1].start()
        done.add(("two", chunk))
        yield (), (), COST[6], None
        dpre = dot_nn(k.dres2_low[all_rows], k.full[DOWN]) * k.slope[all_rows]
        k.bias_acc[chunk] = column_sum(dpre)
        k.dpre_low[all_rows] = dpre.astype(low)
        k.part[SUM_BACK, all_rows] = dot_nt(k.dpre_low[all_rows], k.full[UP]).astype(low)
        done.add(("dpre", chunk))
        copy = send_near(SUM_BACK)
        yield (), (copy,), COST[1], None
        copy = send_far(SUM_BACK, copy)
        yield (), (copy,), COST[7], None
        dhidden = k.dres2[chunk] + take_far(SUM_BACK, copy)
        normed = k.normed1[chunk]
        dres1 = norm_back(dhidden, normed, k.inverse1[chunk], k.norm[1:2])
        k.dres1[chunk] = dres1
        k.dres1_low[own_rows] = dres1.astype(low)
        copy = trade(EX_ONE, k.dres1_low)
        k.norm_acc[chunk, 0:1] = column_sum(dres1)
        k.norm_acc[chunk, 1:2] = column_sum(dhidden * normed)
        k.norm_acc[chunk, 2:3] = column_sum(dhidden)
        done.add(("sums", chunk))
        yield (), (copy,), COST[8], None
        copy[0].wait_recv()
        done.add(("one", chunk))
        dmix = dot_nn(k.dres1_low[all_rows], k.full[ATTN, :, 3 * group :]).astype(low)
        for head in range(HEADS_HERE):
            k.dmix[head, all_rows] = dmix[:, head * HDIM : (head + 1) * HDIM]
        done.add(("dmix", chunk))
        yield ("dqkv",), (), COST[9], None
        k.part[SUM_INPUT, all_rows] = dot_nt(k.dqkv[all_rows], k.full[ATTN]).astype(low)
        copy = send_near(SUM_INPUT)
        yield (), (copy,), COST[1], None
        copy = send_far(SUM_INPUT, copy)
        yield (), (copy,), COST[10], None
        total = k.dres1[chunk] + take_far(SUM_INPUT, copy)
        k.gin[own_rows] = total.astype(low)
        copy = trade(EX_INPUT, k.gin)
        yield (), (copy,), 0.02, None
        copy[0].wait_recv()
        stores.append(pltpu.make_async_copy(k.gin.at[all_rows], k.gin_hbm.at[all_rows], k.store_sem.at[1, chunk]))
        stores[-1].start()

    def turn(left, right, index, columns):
        k.turned[...] = left[...].T
        grad_tile(index, k.turned, right, columns)

    def grad_tile(index, left_t, right, columns):
        def body(step, carry):
            spot = pl.ds(pl.multiple_of(step * 256, 256), 256)
            product = dot_nn(left_t[spot], right[...]).astype(low)
            k.grads[index, spot, columns] = product[:, : columns.size]
            return carry

        lax.fori_loop(0, width // 256, body, 0)

    def grad_down():
        yield every("two"), (), 1.2, None
        turn(k.dres2_low, k.act, DOWN, pl.ds(0, width))
        done.add(("grad", DOWN))

    def grad_up():
        yield every("dpre"), (), 1.2, None
        turn(k.hidden_low, k.dpre_low, UP, pl.ds(0, width))
        done.add(("grad", UP))

    def grad_attn():
        yield every("one"), (), 0.5, None
        turn(k.dres1_low, k.mixed, ATTN, pl.ds(3 * group, group))
        yield ("dqkv",), (), 1.0, None
        grad_tile(ATTN, k.tokens_t, k.dqkv, pl.ds(0, 3 * group))
        done.add(("grad", ATTN))

    def attention_back():
        for head in range(HEADS_HERE):
            yield every("dmix"), (), 1.4, None
            start = head * HDIM
            dkey, dvalue = 0.0, 0.0
            for step in range(rows // 256):
                spot = pl.ds(step * 256, 256)
                dprob = dot_nt(k.value[head], k.dmix[head, spot])
                probs = k.probs[head, :, spot]
                total = jnp.sum(probs * dprob, 0, keepdims=True)
                dscore = (probs * (dprob - total)).astype(low)
                k.dquery_t[start : start + HDIM, spot] = dot_nn(k.key_t[head], dscore)
                dkey += dot_nn(dscore, k.query[head, spot])
                dvalue += dot_nn(probs.astype(low), k.dmix[head, spot])
            k.dqkv[:, group + start : group + start + HDIM] = dkey.astype(low)
            k.dqkv[:, 2 * group + start : 2 * group + start + HDIM] = dvalue.astype(low)
            k.small[1:2, 384 + start : 384 + start + HDIM] = column_sum(dvalue)
        yield (), (), 0.3, None
        dquery = k.dquery_t[...].T
        k.dqkv[:, :group] = dquery.astype(low)
        k.small[0:1, 384 : 384 + group] = column_sum(dquery)
        done.add("dqkv")

    def small_sums():
        yield every("sums"), (), 0.1, None
        norm_total = k.norm_acc[0]
        bias_total = k.bias_acc[0]
        for chunk in range(1, CHUNKS):
            norm_total += k.norm_acc[chunk]
            bias_total += k.bias_acc[chunk]
        half_width = width // 2
        k.norm_half[0] = norm_total[:, :half_width]
        k.norm_half[1] = norm_total[:, half_width:]
        pair = send(
            k.norm_half.at[1 - core],
            k.norm_in,
            k.pair_send.at[0],
            k.pair_recv.at[0],
            {"tensor": partner},
            "near",
            0.05,
        )
        for spot in range(4):
            k.small[2 + spot : 3 + spot, 384 : 384 + group] = bias_total[:, spot * group : (spot + 1) * group]
        yield ("dqkv",), (pair,), 0.2, None
        pair[0].wait_recv()
        k.small[:, :half_width] = k.norm_half[core] + k.norm_in[...]
        shared = [
            send(
                k.small,
                k.slots.at[me],
                k.dp_send.at[shift - 1],
                k.dp_recv.at[shift - 1],
                {"dp": (me + shift) % RING},
                shift % 2,
                0.5,
            )
            for shift in range(1, RING)
        ]
        k.slots[me] = k.small[...]
        yield (), tuple(shared), 0.2, None
        for copy in shared:
            copy[0].wait_recv()
        small_total = k.slots[0]
        for index in range(1, RING):
            small_total += k.slots[index]
        k.bias_out[...] = small_total[:, 384:640]
        k.norm_fin[core] = small_total[:, :half_width]
        pair = send(
            k.norm_fin.at[core],
            k.norm_fin.at[core],
            k.pair_send.at[1],
            k.pair_recv.at[1],
            {"tensor": partner},
            "near",
            0.05,
        )
        yield (), (pair,), 0.05, None
        pair[0].wait_recv()
        k.norm_out[...] = k.norm_fin[...]

    plans = [((3, 0), prepare()), ((2, 0), attention())]
    for index in range(3):
        for half in range(PIECES):
            for way in range(2):
                plans.append(((0, index, half), gather_chain(index, half, way)))
                plans.append(((0, 2 - index, half), scatter_chain(index, half, way)))
    plans += [((2, 1 + chunk), chunk_steps(chunk)) for chunk in range(CHUNKS)]
    plans += [((1, 0), grad_down()), ((2, 9), attention_back()), ((3, 1), grad_up()), ((1, 1), grad_attn())]
    plans.append(((5, 0), small_sums()))
    for index, total in ((DOWN, k.tot2), (UP, k.tot1), (ATTN, k.tot0)):
        for half in range(PIECES):
            plans.append(((4, half), scatter_end(index, half, total)))
    run_all(plans)
    for flight in sent:
        flight[2].wait_send()
    for store in stores:
        store.wait()


def run_layer(tokens, cotangent, lengths, in_weight, out_weight, in_bias, norm_vec):
    rows, width = tokens.shape
    slab, group = in_weight.shape[1:]
    scratch = scratch_list(rows, width, slab, group)
    names = INPUTS + OUTPUTS + tuple(scratch)
    anywhere = pl.BlockSpec(memory_space=pl.ANY)
    inside = pl.BlockSpec(memory_space=pltpu.VMEM)
    scalar = pl.BlockSpec(memory_space=pltpu.SMEM)
    total = jax.ShapeDtypeStruct((slab, width), jnp.float32)
    like = jax.ShapeDtypeStruct((rows, width), jnp.bfloat16)
    return pl.pallas_call(
        functools.partial(layer_kernel, names),
        out_shape=(
            like,
            like,
            total,
            total,
            total,
            jax.ShapeDtypeStruct((2, 8, width // 2), jnp.float32),
            jax.ShapeDtypeStruct((8, 256), jnp.float32),
        ),
        in_specs=[anywhere, anywhere, scalar] + [anywhere] * 4,
        out_specs=(anywhere,) * 2 + (inside,) * (len(OUTPUTS) - 2),
        scratch_shapes=list(scratch.values()),
        compiler_params=pltpu.CompilerParams(
            collective_id=0, has_side_effects=True, vmem_limit_bytes=56 * 2**20
        ),
        name="layer",
    )(tokens, cotangent, lengths, in_weight, out_weight, in_bias, norm_vec)


def scatter_plain(grads):
    share = lax.psum_scatter(grads, "dp", scatter_dimension=0, tiled=True)
    return share.astype(jnp.float32)


def matmul(left_op, right_op):
    return jnp.dot(left_op, right_op, preferred_element_type=jnp.float32)


def inner_rows(left_op, right_op):
    return lax.dot_general(
        left_op, right_op, (((0,), (0,)), ((), ())), preferred_element_type=jnp.float32
    )


def times_transposed(left_op, right_op):
    return lax.dot_general(
        left_op, right_op, (((1,), (1,)), ((), ())), preferred_element_type=jnp.float32
    )


def layer_norm(summed_rows, gain_vec, shift_vec):
    center = jnp.mean(summed_rows, -1, keepdims=True)
    offset = summed_rows - center
    inverse = lax.rsqrt(jnp.mean(offset * offset, -1, keepdims=True) + norm_eps)
    normed = offset * inverse
    return (normed * gain_vec + shift_vec, normed, inverse)


def norm_back(upstream, normed, inverse, gain_vec):
    scaled = upstream * gain_vec
    return inverse * (
        scaled
        - jnp.mean(scaled, -1, keepdims=True)
        - normed * jnp.mean(scaled * normed, -1, keepdims=True)
    )


def gelu_value(pre_act):
    return 0.5 * pre_act * (1.0 + jax.scipy.special.erf(pre_act * root_half))


def gelu_slope(pre_act):
    return (
        0.5 * (1.0 + jax.scipy.special.erf(pre_act * root_half))
        + pre_act * jnp.exp(-0.5 * pre_act * pre_act) * normal_peak
    )


def score_block(query_heads, key_heads, length):
    seq_len = query_heads.shape[0]
    scale_factor = query_heads.shape[-1] ** (-0.5)
    scores = (
        jnp.einsum("qhe,khe->hqk", query_heads, key_heads, preferred_element_type=jnp.float32)
        * scale_factor
    )
    usable = lax.broadcasted_iota(jnp.int32, (1, 1, seq_len), 2) < length
    return jnp.where(usable, scores, masked_score)


def attend_forward(operands):
    query_heads, key_heads, value_heads, length = operands
    scores = score_block(query_heads, key_heads, length)
    highest = jnp.max(scores, -1, keepdims=True)
    log_total = highest + jnp.log(jnp.sum(jnp.exp(scores - highest), -1, keepdims=True))
    probs_low = jnp.exp(scores - log_total).astype(jnp.bfloat16)
    mixed_heads = jnp.einsum(
        "hqk,khe->qhe", probs_low, value_heads, preferred_element_type=jnp.float32
    )
    return (mixed_heads.astype(jnp.bfloat16), log_total)


def attend_backward(operands):
    query_heads, key_heads, value_heads, grad_heads, log_total, length = operands
    scale_factor = query_heads.shape[-1] ** (-0.5)
    scores = score_block(query_heads, key_heads, length)
    probs = jnp.exp(scores - log_total)
    probs_low = probs.astype(jnp.bfloat16)
    grad_probs = jnp.einsum(
        "qhe,khe->hqk", grad_heads, value_heads, preferred_element_type=jnp.float32
    )
    row_dot = jnp.sum(probs * grad_probs, -1, keepdims=True)
    grad_scores = (probs * (grad_probs - row_dot) * scale_factor).astype(jnp.bfloat16)
    grad_query = jnp.einsum(
        "hqk,khe->qhe", grad_scores, key_heads, preferred_element_type=jnp.float32
    )
    grad_keys = jnp.einsum(
        "hqk,qhe->khe", grad_scores, query_heads, preferred_element_type=jnp.float32
    )
    grad_values = jnp.einsum(
        "hqk,qhe->khe", probs_low, grad_heads, preferred_element_type=jnp.float32
    )
    return (grad_query, grad_keys, grad_values)


def adam_update(param, grad, moments, decay):
    first = beta_first * moments[0] + (1.0 - beta_first) * grad
    second = beta_second * moments[1] + (1.0 - beta_second) * grad * grad
    first_hat = first / (1.0 - beta_first**step_count)
    second_hat = second / (1.0 - beta_second**step_count)
    new_param = param - learn_rate * (first_hat / (jnp.sqrt(second_hat) + adam_eps) + decay * param)
    return (new_param, jnp.stack([first, second]))


def adam_store(param, grad, moments, decay, new_param, new_moments):
    first = beta_first * moments[0] + (1.0 - beta_first) * grad
    second = beta_second * moments[1] + (1.0 - beta_second) * grad * grad
    first_hat = first * (1.0 / (1.0 - beta_first**step_count))
    second_hat = second * (1.0 / (1.0 - beta_second**step_count))
    step = first_hat / (jnp.sqrt(second_hat) + adam_eps) + decay * param
    new_param[...] = param - learn_rate * step
    new_moments[0][...] = first
    new_moments[1][...] = second


def adam_kernel(*refs):
    tot0, tot1, tot2, norm_ref, bias_ref, out_from, gin_from = refs[:7]
    params, moments = refs[7:11], refs[11:15]
    out_to, gin_to = refs[15:17]
    grads, new_params, new_moments = refs[17:21], refs[21:25], refs[25:29]
    held = (refs[29:32], refs[32:35])
    fresh = (refs[35:37], refs[37:39])
    pass_ref, pass_sem, in_sem, out_sem = refs[39:]
    width = params[0].shape[2]

    def place_of(index):
        if index == 3 or index >= 8:
            return 1, 0 if index == 3 else index - 7
        return 0, index if index < 3 else index - 1

    loads = [
        [
            pltpu.make_async_copy(params[group], held[group][0], in_sem.at[group, 0]),
            pltpu.make_async_copy(moments[group], held[group][1], in_sem.at[group, 1]),
        ]
        for group in range(2)
    ]
    for group in (1, 0):
        for copy in loads[group]:
            copy.start()
    passing = [
        pltpu.make_async_copy(source, pass_ref.at[spot], pass_sem.at[0, spot])
        for spot, source in enumerate((out_from, gin_from))
    ]
    for copy in passing:
        copy.start()
    stores = []
    for turn, (group, spots, indices) in enumerate(
        ((1, (1, 5), range(8, 12)), (0, (3, 7), range(4, 8)), (1, (0, 1), (3,)), (0, (0, 3), range(3)))
    ):
        if turn < 2:
            for copy in loads[group]:
                copy.wait()
        for index in indices:
            spot = place_of(index)[1]
            place = index % 4
            grad = (tot0, tot1, tot2)[index // 4][:, place * width : (place + 1) * width]
            if group:
                grad = grad.T
            held[group][2][spot] = grad
            adam_store(
                held[group][0][spot],
                grad,
                (held[group][1][0, spot], held[group][1][1, spot]),
                weight_decay,
                fresh[group][0].at[spot],
                (fresh[group][1].at[0, spot], fresh[group][1].at[1, spot]),
            )
        part = pl.ds(spots[0], spots[1] - spots[0])
        results = (
            (held[group][2].at[part], grads[group].at[part]),
            (fresh[group][0].at[part], new_params[group].at[part]),
            (fresh[group][1].at[:, part], new_moments[group].at[:, part]),
        )
        for place, (source, target) in enumerate(results):
            stores.append(pltpu.make_async_copy(source, target, out_sem.at[turn, place]))
            stores[-1].start()
        if turn == 0:
            for spot, target in enumerate((out_to, gin_to)):
                passing[spot].wait()
                stores.append(pltpu.make_async_copy(pass_ref.at[spot], target, pass_sem.at[1, spot]))
                stores[-1].start()
    norm_grad = jnp.concatenate([norm_ref[0, :6], norm_ref[1, :6]], 1)
    for group, grad in ((2, bias_ref[:6, :width]), (3, norm_grad)):
        grads[group][...] = grad
        adam_store(
            params[group][...],
            grad,
            (moments[group][:, 0, :], moments[group][:, 1, :]),
            0.0,
            new_params[group],
            (new_moments[group].at[:, 0, :], new_moments[group].at[:, 1, :]),
        )
    for copy in stores:
        copy.wait()


def update_here(rows, totals, params, moments):
    moments = moments[:2] + tuple(m.swapaxes(0, 1) for m in moments[2:])
    inside = pl.BlockSpec(memory_space=pltpu.VMEM)
    anywhere = pl.BlockSpec(memory_space=pl.ANY)
    kinds = [anywhere, anywhere, inside, inside]
    shapes = [jax.ShapeDtypeStruct(a.shape, jnp.float32) for a in params + params + moments]
    first, second, first_pair, second_pair = params[:2] + moments[:2]
    held = (first, first_pair, first, second, second_pair, second)
    fresh = (first, first_pair, second, second_pair)
    blocks = [pltpu.VMEM(a.shape, jnp.float32) for a in held + fresh]
    dma = pltpu.SemaphoreType.DMA
    results = pl.pallas_call(
        adam_kernel,
        out_shape=tuple(jax.ShapeDtypeStruct(a.shape, a.dtype) for a in rows) + tuple(shapes),
        in_specs=[inside] * len(totals) + [anywhere] * 2 + kinds * 2,
        out_specs=tuple([anywhere] * 2 + kinds * 3),
        scratch_shapes=blocks + [pltpu.VMEM((2,) + rows[0].shape, rows[0].dtype), dma((2, 2)), dma((2, 2)), dma((4, 3))],
        name="adam",
    )(*totals, *rows, *params, *moments)
    return results[:-2] + tuple(m.swapaxes(0, 1) for m in results[-2:])


def update_plain(share, rest, small, params, moments):
    group_width, width = params[0].shape[2], params[3].shape[1]
    total = jnp.concatenate([share, rest], 1)
    blocks = [total[:, k * group_width : (k + 1) * group_width] for k in range(12)]
    grads = (
        jnp.stack(blocks[:3] + blocks[4:8]),
        jnp.stack([blocks[3]] + blocks[8:]).swapaxes(1, 2),
        small[:6, width : width + group_width],
        small[:6, :width],
    )
    decays = (weight_decay, weight_decay, 0.0, 0.0)
    news = [adam_update(*group) for group in zip(params, grads, moments, decays)]
    return grads + tuple(n[0] for n in news) + tuple(n[1] for n in news)


def plain_layer(
    tokens,
    cotangent,
    lengths,
    in_weight,
    out_weight,
    in_bias,
    norm_vec,
    in_moments,
    out_moments,
    bias_moments,
    norm_moments,
):
    seq_count, seq_len, width = tokens.shape
    row_count = seq_count * seq_len
    in_low = in_weight.astype(jnp.bfloat16)
    out_low = out_weight.astype(jnp.bfloat16).swapaxes(1, 2)
    share = jnp.concatenate(list(in_low[:3]) + [out_low[0]], 1)
    rest = jnp.concatenate(list(in_low[3:]) + list(out_low[1:]), 1)
    first_full = lax.all_gather(share, "dp", axis=0, tiled=True)
    second_full = lax.all_gather(rest, "dp", axis=0, tiled=True)
    group_width = in_weight.shape[2]
    heads_here = group_width // HDIM
    w_qkv = first_full[:, : 3 * group_width]
    w_proj = first_full[:, 3 * group_width :]
    bias_up = in_bias[2:6].reshape(1, 4 * group_width)

    def split_heads(flat_rows):
        return flat_rows.reshape(seq_count, seq_len, heads_here, HDIM)

    flat_tokens = tokens.reshape(row_count, width)
    qkv = matmul(flat_tokens, w_qkv)
    query = (qkv[:, :group_width] + in_bias[0]).astype(jnp.bfloat16)
    keys_low = qkv[:, group_width : 2 * group_width].astype(jnp.bfloat16)
    values_low = (qkv[:, 2 * group_width :] + in_bias[1]).astype(jnp.bfloat16)
    mixed_heads, log_total = lax.map(
        attend_forward,
        (split_heads(query), split_heads(keys_low), split_heads(values_low), lengths),
    )
    mixed_flat = mixed_heads.reshape(row_count, group_width)
    attn_part = times_transposed(mixed_flat, w_proj).astype(jnp.bfloat16)
    attn_out = lax.psum(attn_part, "tensor")
    w_up = second_full[:, : 4 * group_width]
    w_down = second_full[:, 4 * group_width :]
    hidden, normed_one, inverse_one = layer_norm(
        flat_tokens.astype(jnp.float32) + attn_out.astype(jnp.float32) + norm_vec[0], norm_vec[1], norm_vec[2]
    )
    hidden_low = hidden.astype(jnp.bfloat16)
    pre_act = matmul(hidden_low, w_up) + bias_up
    act_low = gelu_value(pre_act).astype(jnp.bfloat16)
    ffn_part = times_transposed(act_low, w_down).astype(jnp.bfloat16)
    ffn_out = lax.psum(ffn_part, "tensor").astype(jnp.float32)
    out_rows, normed_two, inverse_two = layer_norm(
        hidden + ffn_out + norm_vec[3], norm_vec[4], norm_vec[5]
    )
    positions = lax.broadcasted_iota(jnp.int32, (seq_count, seq_len), 1)
    live_rows = (positions < lengths[:, None]).astype(jnp.float32).reshape(row_count, 1)
    grad_out = cotangent.reshape(row_count, width).astype(jnp.float32) * live_rows
    grad_two = norm_back(grad_out, normed_two, inverse_two, norm_vec[4])
    grad_two_low = grad_two.astype(jnp.bfloat16)
    grad_down = inner_rows(grad_two_low, act_low).astype(jnp.bfloat16)
    grad_act = matmul(grad_two_low, w_down)
    grad_pre = grad_act * gelu_slope(pre_act)
    grad_pre_low = grad_pre.astype(jnp.bfloat16)
    grad_up = inner_rows(hidden_low, grad_pre_low).astype(jnp.bfloat16)
    rest_grads = jnp.concatenate([grad_up, grad_down], 1)
    back_part = times_transposed(grad_pre_low, w_up).astype(jnp.bfloat16)
    back_sum = lax.psum(back_part, "tensor")
    grad_hidden = grad_two + back_sum.astype(jnp.float32)
    grad_one = norm_back(grad_hidden, normed_one, inverse_one, norm_vec[1])
    grad_one_low = grad_one.astype(jnp.bfloat16)
    grad_proj = inner_rows(grad_one_low, mixed_flat).astype(jnp.bfloat16)
    grad_mixed = matmul(grad_one_low, w_proj).astype(jnp.bfloat16)
    grad_query, grad_keys, grad_values = lax.map(
        attend_backward,
        (
            split_heads(query),
            split_heads(keys_low),
            split_heads(values_low),
            split_heads(grad_mixed),
            log_total,
            lengths,
        ),
    )
    grad_query = grad_query.reshape(row_count, group_width)
    grad_keys = grad_keys.reshape(row_count, group_width)
    grad_values = grad_values.reshape(row_count, group_width)
    qkv_grad_low = jnp.concatenate([grad_query, grad_keys, grad_values], 1).astype(jnp.bfloat16)
    input_part = times_transposed(qkv_grad_low, w_qkv).astype(jnp.bfloat16)
    grad_qkv = inner_rows(flat_tokens, qkv_grad_low).astype(jnp.bfloat16)
    first_grads = jnp.concatenate([grad_qkv, grad_proj], 1)
    bias_rows = jnp.concatenate(
        [jnp.sum(grad_query, 0), jnp.sum(grad_values, 0), jnp.sum(grad_pre, 0)]
    ).reshape(6, group_width)
    norm_rows = jnp.stack(
        [
            jnp.sum(grad_one, 0),
            jnp.sum(grad_hidden * normed_one, 0),
            jnp.sum(grad_hidden, 0),
            jnp.sum(grad_two, 0),
            jnp.sum(grad_out * normed_two, 0),
            jnp.sum(grad_out, 0),
        ]
    )
    small = jnp.pad(jnp.concatenate([norm_rows, bias_rows], 1), ((0, 2), (0, 64)))
    share_total = scatter_plain(first_grads)
    rest_total = scatter_plain(rest_grads)
    input_sum = lax.psum(input_part, "tensor")
    small_total = lax.psum(small, "dp")
    grad_input = grad_one + input_sum.astype(jnp.float32)
    params = (in_weight, out_weight, in_bias, norm_vec)
    moments = (in_moments, out_moments, bias_moments, norm_moments)
    updates = update_plain(share_total, rest_total, small_total, params, moments)
    output = out_rows.astype(jnp.bfloat16).reshape(seq_count, seq_len, width)
    grad_tokens = grad_input.astype(jnp.bfloat16).reshape(seq_count, seq_len, width)
    return (
        output,
        grad_tokens,
    ) + tuple(updates)


def local(*operands):
    tokens, cotangent, lengths, in_weight, out_weight, in_bias, norm_vec = operands[:7]
    ring = lax.axis_size("dp") == RING and lax.axis_size("tensor") == 4
    if not ring or tokens.shape[0] != 1:
        return plain_layer(*operands)
    out, grad_tokens, *totals = run_layer(
        tokens[0], cotangent[0], lengths, in_weight, out_weight, in_bias, norm_vec
    )
    results = update_here((out, grad_tokens), tuple(totals), operands[3:7], operands[7:])
    return (results[0][None], results[1][None]) + tuple(results[2:])


def solution(mesh):
    in_specs = (
        P("dp", None, None),
        P("dp", None, None),
        P("dp"),
        P(None, "dp", "tensor"),
        P(None, "tensor", "dp"),
        P(None, "tensor"),
        P(),
        P(None, None, "dp", "tensor"),
        P(None, None, "tensor", "dp"),
        P(None, None, "tensor"),
        P(),
    )
    out_specs = (
        P("dp", None, None),
        P("dp", None, None),
        P(None, "dp", "tensor"),
        P(None, "tensor", "dp"),
        P(None, "tensor"),
        P(),
        P(None, "dp", "tensor"),
        P(None, "tensor", "dp"),
        P(None, "tensor"),
        P(),
        P(None, None, "dp", "tensor"),
        P(None, None, "tensor", "dp"),
        P(None, None, "tensor"),
        P(),
    )
    return jax.shard_map(local, mesh=mesh, in_specs=in_specs, out_specs=out_specs, check_vma=False)
```

```python
import functools

import jax
import jax.numpy as jnp
from jax import lax
from jax.experimental import pallas as pl
from jax.experimental.pallas import tpu as pltpu
from jax.sharding import PartitionSpec as P

HDIM = 64


norm_eps = 1e-12
masked_score = -1e30
learn_rate = 0.005
beta_first = 0.9
beta_second = 0.999
adam_eps = 1e-08
weight_decay = 0.01
step_count = 2.0
root_half = 0.7071067811865476
normal_peak = 0.3989422804014327


RING = 8
CHUNKS = 2
PIECES = 3
PIECE_TIME = 3.2 / PIECES
LINK_DELAY = {"near": 1.5, "far": 2.2, 0: 2.0, 1: 2.0}
FILL_LIMIT = (0.3, 2.0, 3.0)
SLAB_ORDER = (4, 3, 5, 2, 6, 1, 7, 0)
WAIT_TIME = 0.06
SCATTER_LIMIT = 99.0
COST = [c * 3.6 / CHUNKS for c in (0.2, 0.1, 0.25, 0.6, 0.3, 0.45, 0.6, 0.35, 0.2, 0.3, 0.15)]
HEADS_HERE = 3
MESH = pl.DeviceIdType.MESH
ATTN, UP, DOWN = 0, 1, 2
SUM_ATTN, SUM_FFN, SUM_BACK, SUM_INPUT = 0, 1, 2, 3
EX_HIDDEN, EX_OUT, EX_TWO, EX_ONE, EX_INPUT = 0, 1, 2, 3, 4


def ring_place(index):
    depth, side = index // 2, index % 2
    return depth + side * (RING - 1 - 2 * depth)


def ring_device(place):
    side = place // (RING // 2)
    depth = place + side * (RING - 1 - 2 * place)
    return 2 * depth + side


def dot_nn(left_op, right_op):
    return jnp.dot(left_op, right_op, preferred_element_type=jnp.float32)


def dot_nt(left_op, right_op):
    return lax.dot_general(
        left_op, right_op, (((1,), (1,)), ((), ())), preferred_element_type=jnp.float32
    )


def normalize(rows):
    center = jnp.mean(rows, -1, keepdims=True)
    offset = rows - center
    inverse = lax.rsqrt(jnp.mean(offset * offset, -1, keepdims=True) + norm_eps)
    return offset * inverse, inverse


def hops(index, half, way):
    return 3 + (half + way + 1 + index) % 2


def column_sum(rows):
    return jnp.sum(rows, 0, keepdims=True)


INPUTS = ("tokens_hbm", "cot_hbm", "lengths", "inw_hbm", "outw_hbm", "bias_hbm", "norm_hbm")
OUTPUTS = ("out_hbm", "gin_hbm", "tot0", "tot1", "tot2", "norm_out", "bias_out")


def scratch_list(rows, width, slab, group):
    own = rows // (2 * CHUNKS)
    piece = slab // PIECES
    low, wide = jnp.bfloat16, jnp.float32
    dma = pltpu.SemaphoreType.DMA
    vmem = pltpu.VMEM
    heads = (HEADS_HERE, rows, HDIM)
    turned = (HEADS_HERE, HDIM, rows)
    return {
        "tokens": vmem((rows, width), low),
        "out": vmem((rows, width), low),
        "gin": vmem((rows, width), low),
        "store_sem": dma((2, CHUNKS)),
        "cot": vmem((rows, width), low),
        "inw": vmem((7, slab, group), wide),
        "outw": vmem((5, group, slab), wide),
        "bias": vmem((6, group), wide),
        "norm": vmem((6, width), wide),
        "full": vmem((3, width, width), low),
        "grads": vmem((3, width, width), low),
        "arrived": vmem((3, 4, PIECES, 2, piece, width), low),
        "leaving": vmem((3, 4, PIECES, 2, piece, width), low),
        "tokens_t": vmem((width, rows), low),
        "qkv_bias": vmem((1, width), wide),
        "up_bias": vmem((1, width), wide),
        "query": vmem(heads, low),
        "key": vmem(heads, low),
        "value": vmem(heads, low),
        "dmix": vmem(heads, low),
        "key_t": vmem(turned, low),
        "value_t": vmem(turned, low),
        "probs": vmem((HEADS_HERE, rows, rows), wide),
        "mixed_t": vmem((group, rows), low),
        "mixed": vmem((rows, group), low),
        "dkey": vmem(heads, wide),
        "dvalue": vmem(heads, wide),
        "dquery_t": vmem((group, rows), wide),
        "dqkv": vmem((rows, width), low),
        "part": vmem((4, rows, width), low),
        "near": vmem((4, CHUNKS, own, width), low),
        "chip": vmem((4, CHUNKS, own, width), low),
        "far": vmem((4, CHUNKS, own, width), low),
        "hidden": vmem((CHUNKS, own, width), wide),
        "normed1": vmem((CHUNKS, own, width), wide),
        "inverse1": vmem((CHUNKS, own, 1), wide),
        "dres2": vmem((CHUNKS, own, width), wide),
        "dres1": vmem((CHUNKS, own, width), wide),
        "hidden_low": vmem((rows, width), low),
        "dres2_low": vmem((rows, width), low),
        "dres1_low": vmem((rows, width), low),
        "act": vmem((rows, width), low),
        "slope": vmem((rows, width), wide),
        "dpre_low": vmem((rows, width), low),
        "norm_acc": vmem((CHUNKS, 8, width), wide),
        "bias_acc": vmem((CHUNKS, 1, width), wide),
        "norm_half": vmem((2, 8, width // 2), wide),
        "norm_in": vmem((8, width // 2), wide),
        "small": vmem((8, 640), wide),
        "norm_fin": vmem((2, 8, width // 2), wide),
        "turned": vmem((width, rows), low),
        "turned_up": vmem((width, rows), low),
        "turned_attn": vmem((width, rows), low),
        "slots": vmem((RING, 8, 640), wide),
        "load_sem": dma((8,)),
        "g_send": dma((3, 4, PIECES, 2)),
        "g_recv": dma((3, 4, PIECES, 2)),
        "s_send": dma((3, 4, PIECES, 2)),
        "s_recv": dma((3, 4, PIECES, 2)),
        "near_send": dma((4, CHUNKS)),
        "near_recv": dma((4, CHUNKS)),
        "far_send": dma((4, CHUNKS)),
        "far_recv": dma((4, CHUNKS)),
        "ex_send": dma((5, CHUNKS)),
        "ex_recv": dma((5, CHUNKS)),
        "dp_send": dma((RING - 1,)),
        "dp_recv": dma((RING - 1,)),
        "pair_send": dma((2,)),
        "pair_recv": dma((2,)),
    }


class Names:
    pass


def layer_kernel(names, *refs):
    k = Names()
    for name, ref in zip(names, refs):
        setattr(k, name, ref)
    rows, width = k.tokens.shape
    group, slab = k.bias.shape[1], k.inw.shape[1]
    span = rows // CHUNKS
    own = span // 2
    piece = slab // PIECES
    low, wide = jnp.bfloat16, jnp.float32
    me, tensor = lax.axis_index("dp"), lax.axis_index("tensor")
    core = tensor % 2
    partner, across = tensor + 1 - 2 * core, (tensor + 2) % 4
    place = ring_place(me)
    targets = (ring_device((place + 1) % RING), ring_device((place + RING - 1) % RING))
    passed, stores, sent, done, free = [], [], [], set(), dict.fromkeys(("near", "far", 0, 1), 0.0)
    clock = [0.0]

    def send(source, target, send_sem, recv_sem, device, link, busy):
        copy = pltpu.make_async_remote_copy(
            src_ref=source,
            dst_ref=target,
            send_sem=send_sem,
            recv_sem=recv_sem,
            device_id=device,
            device_id_type=MESH,
        )
        copy.start()
        free[link] = max(free[link], clock[0]) + busy
        sent.append((free[link] + LINK_DELAY[link], len(sent), copy))
        return copy, free[link] + LINK_DELAY[link]

    def run_all(plans):
        active = [[rank, plan, next(plan)] for rank, plan in plans]
        while active:
            best = None
            for item in active:
                rank, plan, (flags, flights, cost, gate) = item
                if any(flag not in done for flag in flags):
                    continue
                ready = max([clock[0]] + [flight[1] for flight in flights])
                if gate:
                    limit = gate[1] if gate[2] else FILL_LIMIT[min(len(passed) // (2 * PIECES), 2)]
                    ready = max(ready, free[gate[0]] - limit)
                if best is None or (ready, rank) < best[0]:
                    best = (ready, rank), item
            (ready, rank), item = best
            turns = int((ready - clock[0]) / WAIT_TIME)
            for flight in sorted(sent)[:turns]:
                if flight[0] <= clock[0]:
                    flight[2].wait_send()
                    sent.remove(flight)
            clock[0] = ready + item[2][2]
            item[2] = next(item[1], None)
            if item[2] is None:
                active.remove(item)

    def slab_rows(owner, half):
        return pl.ds(pl.multiple_of(owner * slab + half * piece, piece), piece)

    def gather_chain(index, half, way):
        length = hops(index, half, way)
        flight = None
        for step in range(length):
            shift = RING - step if way == 0 else step
            spot = k.full.at[index, slab_rows(ring_device((place + shift) % RING), half)]
            spots = (index, step, half, way)
            gate = (way, 99.0, index == ATTN)
            if step:
                yield (), (flight,), 0.05, gate
                flight[0].wait_recv()
            else:
                yield (("own", index),), (), 0.05, gate
            flight = send(
                spot, spot, k.g_send.at[spots], k.g_recv.at[spots], {"dp": targets[way]}, way, PIECE_TIME
            )
        passed.append(index)
        yield (), (flight,), 0.02, None
        flight[0].wait_recv()
        done.add(("full", index, half, way))

    def all_of(index):
        return tuple(("full", index, half, way) for half in range(PIECES) for way in range(2))

    def every(name):
        return tuple((name, chunk) for chunk in range(CHUNKS))

    ends = {}

    def scatter_chain(index, half, way):
        length = hops(index, half, way)
        flight = None
        for step in range(length):
            shift = length - step if way == 0 else RING - length + step
            spot = (index, slab_rows(ring_device((place + shift) % RING), half))
            spots = (index, step, half, way)
            gate = (way, SCATTER_LIMIT, True)
            if step:
                yield (("grad", index, shift),), (flight,), 0.08, gate
                flight[0].wait_recv()
                come = k.arrived[index, step - 1, half, way].astype(wide)
                k.leaving[spots] = (come + k.grads[spot].astype(wide)).astype(low)
                source = k.leaving.at[spots]
            else:
                yield (("grad", index, shift),), (), 0.05, gate
                source = k.grads.at[spot]
            flight = send(
                source,
                k.arrived.at[spots],
                k.s_send.at[spots],
                k.s_recv.at[spots],
                {"dp": targets[way]},
                way,
                PIECE_TIME,
            )
        ends[index, half, way] = flight
        done.add(("end", index, half, way))

    def scatter_end(index, half, total):
        needed = tuple(("end", index, half, way) for way in range(2))
        yield needed + (("grad", index, 0),), (), 0.0, None
        yield (), tuple(ends[index, half, way] for way in range(2)), 0.1, None
        mine = k.grads[index, slab_rows(me, half)].astype(wide)
        for way in range(2):
            ends[index, half, way][0].wait_recv()
            mine += k.arrived[index, hops(index, half, way) - 1, half, way].astype(wide)
        total[half * piece : (half + 1) * piece] = mine

    loads = [
        pltpu.make_async_copy(source, target, k.load_sem.at[spot])
        for spot, (source, target) in enumerate(
            (
                (k.inw_hbm.at[:3], k.inw.at[:3]),
                (k.outw_hbm.at[:1], k.outw.at[:1]),
                (k.inw_hbm.at[3:], k.inw.at[3:]),
                (k.outw_hbm.at[1:], k.outw.at[1:]),
                (k.tokens_hbm, k.tokens),
                (k.bias_hbm, k.bias),
                (k.norm_hbm, k.norm),
                (k.cot_hbm, k.cot),
            )
        )
    ]
    for load in loads:
        load.start()
    barrier = pltpu.get_barrier_semaphore()
    greeted = [{"dp": (me + shift) % RING} for shift in range(1, RING)]
    greeted += [{"tensor": partner}, {"tensor": across}]
    for device in greeted:
        pl.semaphore_signal(barrier, inc=1, device_id=device, device_id_type=MESH)
    mine = pl.ds(pl.multiple_of(me * slab, slab), slab)

    def lower(index, first, blocks):
        for place_at, block in enumerate(blocks):
            start = (first + place_at) * group
            k.full[index, mine, start : start + group] = block.astype(low)
        done.add(("own", index))

    def prepare():
        yield (), (), 2.0, None
        loads[0].wait()
        loads[1].wait()
        lower(ATTN, 0, [k.inw[spot] for spot in range(3)] + [k.outw[0].T])
        pl.semaphore_wait(barrier, len(greeted))
        yield (), (), 0.4, None
        loads[2].wait()
        lower(UP, 0, [k.inw[3 + spot] for spot in range(4)])
        yield (), (), 0.6, None
        loads[3].wait()
        lower(DOWN, 0, [k.outw[1 + spot].T for spot in range(4)])
        yield (), (), 0.6, None
        for load in loads[4:]:
            load.wait()
        k.qkv_bias[...] = jnp.zeros_like(k.qkv_bias)
        k.qkv_bias[:, :group] = k.bias[0:1]
        k.qkv_bias[:, 2 * group : 3 * group] = k.bias[1:2]
        for spot in range(4):
            k.up_bias[:, spot * group : (spot + 1) * group] = k.bias[2 + spot : 3 + spot]
        k.dqkv[:, 3 * group :] = jnp.zeros((rows, width - 3 * group), low)
        k.small[...] = jnp.zeros_like(k.small)
        k.tokens_t[...] = k.tokens[...].T
        done.add("ready")

    def project(step, carry):
        spot = pl.ds(pl.multiple_of(step * 256, 256), 256)
        qkv = dot_nn(k.tokens[spot], k.full[ATTN]) + k.qkv_bias[...]
        for head in range(HEADS_HERE):
            start = head * HDIM
            k.query[head, spot] = (qkv[:, start : start + HDIM].astype(low) * HDIM**-0.5).astype(low)
            start += group
            k.key[head, spot] = qkv[:, start : start + HDIM].astype(low)
            start += group
            k.value[head, spot] = qkv[:, start : start + HDIM].astype(low)
        return carry

    length = k.lengths[0]

    def attention():
        yield all_of(ATTN) + ("ready",), (), 0.8, None
        lax.fori_loop(0, rows // 256, project, 0)
        yield (), (), 0.3, None
        usable = lax.broadcasted_iota(jnp.int32, (rows, 256), 0) < length
        for head in range(HEADS_HERE):
            k.value_t[head] = k.value[head].T
            k.key_t[head] = (k.key[head] * HDIM**-0.5).astype(low).T
        for head in range(HEADS_HERE):

            def attend(step, carry, head=head):
                spot = pl.ds(pl.multiple_of(step * 256, 256), 256)
                scores = jnp.where(usable, dot_nt(k.key[head], k.query[head, spot]), masked_score)
                highest = jnp.max(scores, 0, keepdims=True)
                raised = jnp.exp(scores - highest)
                probs = raised * (1.0 / jnp.sum(raised, 0, keepdims=True))
                k.probs[head, :, spot] = probs
                mixed = dot_nn(k.value_t[head], probs.astype(low))
                k.mixed_t[head * HDIM : (head + 1) * HDIM, spot] = mixed.astype(low)
                return carry

            yield (), (), 0.9, None
            lax.fori_loop(0, rows // 256, attend, 0)
        yield (), (), 0.15, None
        k.mixed[...] = k.mixed_t[...].T
        done.add("mixed")

    def chunk_steps(chunk):
        all_rows = pl.ds(chunk * span, span)
        own_rows = pl.ds(pl.multiple_of(chunk * span + core * own, own), own)
        other_rows = pl.ds(pl.multiple_of(chunk * span + (1 - core) * own, own), own)

        def send_near(which):
            spots = (which, chunk)
            return send(
                k.part.at[which, other_rows],
                k.near.at[spots],
                k.near_send.at[spots],
                k.near_recv.at[spots],
                {"tensor": partner},
                "near",
                0.2 * 4 / CHUNKS,
            )

        def send_far(which, copy):
            spots = (which, chunk)
            copy[0].wait_recv()
            both = k.near[spots].astype(wide) + k.part[which, own_rows].astype(wide)
            k.chip[spots] = both.astype(low)
            return send(
                k.chip.at[spots],
                k.far.at[spots],
                k.far_send.at[spots],
                k.far_recv.at[spots],
                {"tensor": across},
                "far",
                2.1 * 4 / CHUNKS,
            )

        def take_far(which, copy):
            copy[0].wait_recv()
            return k.chip[which, chunk].astype(wide) + k.far[which, chunk].astype(wide)

        def trade(which, ref):
            spots = (which, chunk)
            return send(
                ref.at[own_rows],
                ref.at[own_rows],
                k.ex_send.at[spots],
                k.ex_recv.at[spots],
                {"tensor": partner},
                "near",
                0.2 * 4 / CHUNKS,
            )

        yield ("mixed",), (), COST[0], None
        k.part[SUM_ATTN, all_rows] = dot_nt(k.mixed[all_rows], k.full[ATTN, :, 3 * group :]).astype(low)
        copy = send_near(SUM_ATTN)
        yield (), (copy,), COST[1], None
        copy = send_far(SUM_ATTN, copy)
        yield (), (copy,), COST[2], None
        attn = take_far(SUM_ATTN, copy)
        normed, inverse = normalize(k.tokens[own_rows].astype(wide) + attn + k.norm[0:1])
        k.normed1[chunk] = normed
        k.inverse1[chunk] = inverse
        hidden = normed * k.norm[1:2] + k.norm[2:3]
        k.hidden[chunk] = hidden
        k.hidden_low[own_rows] = hidden.astype(low)
        copy = trade(EX_HIDDEN, k.hidden_low)
        yield all_of(UP), (copy,), COST[3], None
        copy[0].wait_recv()
        pre = dot_nn(k.hidden_low[all_rows], k.full[UP]) + k.up_bias[...]
        below = 0.5 * (1.0 + lax.erf(pre * root_half))
        k.act[all_rows] = (pre * below).astype(low)
        k.slope[all_rows] = below + pre * jnp.exp(-0.5 * pre * pre) * normal_peak
        yield all_of(DOWN), (), COST[4], None
        k.part[SUM_FFN, all_rows] = dot_nt(k.act[all_rows], k.full[DOWN]).astype(low)
        copy = send_near(SUM_FFN)
        yield (), (copy,), COST[1], None
        copy = send_far(SUM_FFN, copy)
        yield (), (copy,), COST[5], None
        ffn = take_far(SUM_FFN, copy)
        normed, inverse = normalize(k.hidden[chunk] + ffn + k.norm[3:4])
        positions = lax.broadcasted_iota(jnp.int32, (own, 1), 0) + (chunk * span + core * own)
        dout = k.cot[own_rows].astype(wide) * (positions < length).astype(wide)
        dres2 = norm_back(dout, normed, inverse, k.norm[4:5])
        k.dres2[chunk] = dres2
        k.dres2_low[own_rows] = dres2.astype(low)
        two_copy = trade(EX_TWO, k.dres2_low)
        k.out[own_rows] = (normed * k.norm[4:5] + k.norm[5:6]).astype(low)
        out_copy = trade(EX_OUT, k.out)
        k.norm_acc[chunk, 3:4] = column_sum(dres2)
        k.norm_acc[chunk, 4:5] = column_sum(dout * normed)
        k.norm_acc[chunk, 5:6] = column_sum(dout)
        k.norm_acc[chunk, 6:8] = jnp.zeros((2, width), wide)
        yield (), (two_copy,), 0.02, None
        two_copy[0].wait_recv()
        done.add(("two", chunk))
        yield (), (), COST[6], None
        dpre = dot_nn(k.dres2_low[all_rows], k.full[DOWN]) * k.slope[all_rows]
        k.dpre_low[all_rows] = dpre.astype(low)
        k.part[SUM_BACK, all_rows] = dot_nt(k.dpre_low[all_rows], k.full[UP]).astype(low)
        done.add(("dpre", chunk))
        copy = send_near(SUM_BACK)
        k.bias_acc[chunk] = column_sum(dpre)
        yield (), (copy,), COST[1], None
        copy = send_far(SUM_BACK, copy)
        yield (), (out_copy, copy), COST[7], None
        out_copy[0].wait_recv()
        stores.append(pltpu.make_async_copy(k.out.at[all_rows], k.out_hbm.at[all_rows], k.store_sem.at[0, chunk]))
        stores[-1].start()
        dhidden = k.dres2[chunk] + take_far(SUM_BACK, copy)
        normed = k.normed1[chunk]
        dres1 = norm_back(dhidden, normed, k.inverse1[chunk], k.norm[1:2])
        k.dres1[chunk] = dres1
        k.dres1_low[own_rows] = dres1.astype(low)
        copy = trade(EX_ONE, k.dres1_low)
        k.norm_acc[chunk, 0:1] = column_sum(dres1)
        k.norm_acc[chunk, 1:2] = column_sum(dhidden * normed)
        k.norm_acc[chunk, 2:3] = column_sum(dhidden)
        done.add(("sums", chunk))
        yield (), (copy,), COST[8], None
        copy[0].wait_recv()
        done.add(("one", chunk))
        dmix = dot_nn(k.dres1_low[all_rows], k.full[ATTN, :, 3 * group :]).astype(low)
        for head in range(HEADS_HERE):
            k.dmix[head, all_rows] = dmix[:, head * HDIM : (head + 1) * HDIM]
        done.add(("dmix", chunk))
        yield ("dqkv",), (), COST[9], None
        k.part[SUM_INPUT, all_rows] = dot_nt(k.dqkv[all_rows], k.full[ATTN]).astype(low)
        copy = send_near(SUM_INPUT)
        yield (), (copy,), COST[1], None
        copy = send_far(SUM_INPUT, copy)
        yield (), (copy,), COST[10], None
        total = k.dres1[chunk] + take_far(SUM_INPUT, copy)
        k.gin[own_rows] = total.astype(low)
        copy = trade(EX_INPUT, k.gin)
        yield (), (copy,), 0.02, None
        copy[0].wait_recv()
        stores.append(pltpu.make_async_copy(k.gin.at[all_rows], k.gin_hbm.at[all_rows], k.store_sem.at[1, chunk]))
        stores[-1].start()

    def turn(left, right, index, columns):
        k.turned_attn[...] = left[...].T
        grad_tile(index, k.turned_attn, right, columns)

    def grad_tile(index, left_t, right, columns):
        def body(step, carry):
            spot = pl.ds(pl.multiple_of(step * 256, 256), 256)
            product = dot_nn(left_t[spot], right[...]).astype(low)
            k.grads[index, spot, columns] = product[:, : columns.size]
            return carry

        lax.fori_loop(0, width // 256, body, 0)

    def grad_slabs(index, left_t, right, columns):
        for shift in SLAB_ORDER:
            yield (), (), 0.2, None
            owner = ring_device((place + shift) % RING)
            spot = pl.ds(pl.multiple_of(owner * slab, slab), slab)
            product = dot_nn(left_t[spot], right[...]).astype(low)
            k.grads[index, spot, columns] = product[:, : columns.size]
            done.add(("grad", index, shift))

    def grad_down():
        yield every("two"), (), 0.3, None
        k.turned[...] = k.dres2_low[...].T
        yield from grad_slabs(DOWN, k.turned, k.act, pl.ds(0, width))

    def grad_up():
        yield every("dpre"), (), 0.3, None
        k.turned_up[...] = k.hidden_low[...].T
        yield from grad_slabs(UP, k.turned_up, k.dpre_low, pl.ds(0, width))

    def grad_attn():
        yield every("one"), (), 0.5, None
        turn(k.dres1_low, k.mixed, ATTN, pl.ds(3 * group, group))
        yield ("dqkv",), (), 0.02, None
        yield from grad_slabs(ATTN, k.tokens_t, k.dqkv, pl.ds(0, 3 * group))

    def attention_back():
        for step in range(rows // 256):
            needed = tuple(("dmix", chunk) for chunk in range(CHUNKS) if chunk * span < (step + 1) * 256)
            spot = pl.ds(step * 256, 256)
            for head in range(HEADS_HERE):
                yield needed, (), 0.7, None
                start = head * HDIM
                dprob = dot_nt(k.value[head], k.dmix[head, spot])
                probs = k.probs[head, :, spot]
                total = jnp.sum(probs * dprob, 0, keepdims=True)
                dscore = (probs * (dprob - total)).astype(low)
                k.dquery_t[start : start + HDIM, spot] = dot_nn(k.key_t[head], dscore)
                dkey = dot_nn(dscore, k.query[head, spot])
                dvalue = dot_nn(probs.astype(low), k.dmix[head, spot])
                if step:
                    dkey += k.dkey[head]
                    dvalue += k.dvalue[head]
                if step < rows // 256 - 1:
                    k.dkey[head] = dkey
                    k.dvalue[head] = dvalue
                    continue
                k.dqkv[:, group + start : group + start + HDIM] = dkey.astype(low)
                k.dqkv[:, 2 * group + start : 2 * group + start + HDIM] = dvalue.astype(low)
                k.small[1:2, 384 + start : 384 + start + HDIM] = column_sum(dvalue)
        yield (), (), 0.3, None
        dquery = k.dquery_t[...].T
        k.dqkv[:, :group] = dquery.astype(low)
        k.small[0:1, 384 : 384 + group] = column_sum(dquery)
        done.add("dqkv")

    def small_sums():
        yield every("sums"), (), 0.1, None
        norm_total = k.norm_acc[0]
        bias_total = k.bias_acc[0]
        for chunk in range(1, CHUNKS):
            norm_total += k.norm_acc[chunk]
            bias_total += k.bias_acc[chunk]
        half_width = width // 2
        k.norm_half[0] = norm_total[:, :half_width]
        k.norm_half[1] = norm_total[:, half_width:]
        pair = send(
            k.norm_half.at[1 - core],
            k.norm_in,
            k.pair_send.at[0],
            k.pair_recv.at[0],
            {"tensor": partner},
            "near",
            0.05,
        )
        for spot in range(4):
            k.small[2 + spot : 3 + spot, 384 : 384 + group] = bias_total[:, spot * group : (spot + 1) * group]
        yield ("dqkv",), (pair,), 0.2, None
        pair[0].wait_recv()
        k.small[:, :half_width] = k.norm_half[core] + k.norm_in[...]
        shared = [
            send(
                k.small,
                k.slots.at[me],
                k.dp_send.at[shift - 1],
                k.dp_recv.at[shift - 1],
                {"dp": (me + shift) % RING},
                shift % 2,
                0.5,
            )
            for shift in range(1, RING)
        ]
        k.slots[me] = k.small[...]
        yield (), tuple(shared), 0.2, None
        for copy in shared:
            copy[0].wait_recv()
        small_total = k.slots[0]
        for index in range(1, RING):
            small_total += k.slots[index]
        k.bias_out[...] = small_total[:, 384:640]
        k.norm_fin[core] = small_total[:, :half_width]
        pair = send(
            k.norm_fin.at[core],
            k.norm_fin.at[core],
            k.pair_send.at[1],
            k.pair_recv.at[1],
            {"tensor": partner},
            "near",
            0.05,
        )
        yield (), (pair,), 0.05, None
        pair[0].wait_recv()
        k.norm_out[...] = k.norm_fin[...]

    plans = [((3, 0), prepare()), ((2, 0), attention())]
    for index in range(3):
        for half in range(PIECES):
            for way in range(2):
                plans.append(((0, index, half), gather_chain(index, half, way)))
                plans.append(((0, 2 - index, half), scatter_chain(index, half, way)))
    plans += [((2, 1 + chunk), chunk_steps(chunk)) for chunk in range(CHUNKS)]
    plans += [((1, 0), grad_down()), ((2, 9), attention_back()), ((3, 1), grad_up()), ((1, 1), grad_attn())]
    plans.append(((5, 0), small_sums()))
    for index, total in ((DOWN, k.tot2), (UP, k.tot1), (ATTN, k.tot0)):
        for half in range(PIECES):
            plans.append(((4, half), scatter_end(index, half, total)))
    run_all(plans)
    for flight in sent:
        flight[2].wait_send()
    for store in stores:
        store.wait()


def run_layer(tokens, cotangent, lengths, in_weight, out_weight, in_bias, norm_vec):
    rows, width = tokens.shape
    slab, group = in_weight.shape[1:]
    scratch = scratch_list(rows, width, slab, group)
    names = INPUTS + OUTPUTS + tuple(scratch)
    anywhere = pl.BlockSpec(memory_space=pl.ANY)
    inside = pl.BlockSpec(memory_space=pltpu.VMEM)
    scalar = pl.BlockSpec(memory_space=pltpu.SMEM)
    total = jax.ShapeDtypeStruct((slab, width), jnp.float32)
    like = jax.ShapeDtypeStruct((rows, width), jnp.bfloat16)
    return pl.pallas_call(
        functools.partial(layer_kernel, names),
        out_shape=(
            like,
            like,
            total,
            total,
            total,
            jax.ShapeDtypeStruct((2, 8, width // 2), jnp.float32),
            jax.ShapeDtypeStruct((8, 256), jnp.float32),
        ),
        in_specs=[anywhere, anywhere, scalar] + [anywhere] * 4,
        out_specs=(anywhere,) * 2 + (inside,) * (len(OUTPUTS) - 2),
        scratch_shapes=list(scratch.values()),
        compiler_params=pltpu.CompilerParams(
            collective_id=0, has_side_effects=True, vmem_limit_bytes=56 * 2**20
        ),
        name="layer",
    )(tokens, cotangent, lengths, in_weight, out_weight, in_bias, norm_vec)


def scatter_plain(grads):
    share = lax.psum_scatter(grads, "dp", scatter_dimension=0, tiled=True)
    return share.astype(jnp.float32)


def matmul(left_op, right_op):
    return jnp.dot(left_op, right_op, preferred_element_type=jnp.float32)


def inner_rows(left_op, right_op):
    return lax.dot_general(
        left_op, right_op, (((0,), (0,)), ((), ())), preferred_element_type=jnp.float32
    )


def times_transposed(left_op, right_op):
    return lax.dot_general(
        left_op, right_op, (((1,), (1,)), ((), ())), preferred_element_type=jnp.float32
    )


def layer_norm(summed_rows, gain_vec, shift_vec):
    center = jnp.mean(summed_rows, -1, keepdims=True)
    offset = summed_rows - center
    inverse = lax.rsqrt(jnp.mean(offset * offset, -1, keepdims=True) + norm_eps)
    normed = offset * inverse
    return (normed * gain_vec + shift_vec, normed, inverse)


def norm_back(upstream, normed, inverse, gain_vec):
    scaled = upstream * gain_vec
    return inverse * (
        scaled
        - jnp.mean(scaled, -1, keepdims=True)
        - normed * jnp.mean(scaled * normed, -1, keepdims=True)
    )


def gelu_value(pre_act):
    return 0.5 * pre_act * (1.0 + jax.scipy.special.erf(pre_act * root_half))


def gelu_slope(pre_act):
    return (
        0.5 * (1.0 + jax.scipy.special.erf(pre_act * root_half))
        + pre_act * jnp.exp(-0.5 * pre_act * pre_act) * normal_peak
    )


def score_block(query_heads, key_heads, length):
    seq_len = query_heads.shape[0]
    scale_factor = query_heads.shape[-1] ** (-0.5)
    scores = (
        jnp.einsum("qhe,khe->hqk", query_heads, key_heads, preferred_element_type=jnp.float32)
        * scale_factor
    )
    usable = lax.broadcasted_iota(jnp.int32, (1, 1, seq_len), 2) < length
    return jnp.where(usable, scores, masked_score)


def attend_forward(operands):
    query_heads, key_heads, value_heads, length = operands
    scores = score_block(query_heads, key_heads, length)
    highest = jnp.max(scores, -1, keepdims=True)
    log_total = highest + jnp.log(jnp.sum(jnp.exp(scores - highest), -1, keepdims=True))
    probs_low = jnp.exp(scores - log_total).astype(jnp.bfloat16)
    mixed_heads = jnp.einsum(
        "hqk,khe->qhe", probs_low, value_heads, preferred_element_type=jnp.float32
    )
    return (mixed_heads.astype(jnp.bfloat16), log_total)


def attend_backward(operands):
    query_heads, key_heads, value_heads, grad_heads, log_total, length = operands
    scale_factor = query_heads.shape[-1] ** (-0.5)
    scores = score_block(query_heads, key_heads, length)
    probs = jnp.exp(scores - log_total)
    probs_low = probs.astype(jnp.bfloat16)
    grad_probs = jnp.einsum(
        "qhe,khe->hqk", grad_heads, value_heads, preferred_element_type=jnp.float32
    )
    row_dot = jnp.sum(probs * grad_probs, -1, keepdims=True)
    grad_scores = (probs * (grad_probs - row_dot) * scale_factor).astype(jnp.bfloat16)
    grad_query = jnp.einsum(
        "hqk,khe->qhe", grad_scores, key_heads, preferred_element_type=jnp.float32
    )
    grad_keys = jnp.einsum(
        "hqk,qhe->khe", grad_scores, query_heads, preferred_element_type=jnp.float32
    )
    grad_values = jnp.einsum(
        "hqk,qhe->khe", probs_low, grad_heads, preferred_element_type=jnp.float32
    )
    return (grad_query, grad_keys, grad_values)


def adam_update(param, grad, moments, decay):
    first = beta_first * moments[0] + (1.0 - beta_first) * grad
    second = beta_second * moments[1] + (1.0 - beta_second) * grad * grad
    first_hat = first / (1.0 - beta_first**step_count)
    second_hat = second / (1.0 - beta_second**step_count)
    new_param = param - learn_rate * (first_hat / (jnp.sqrt(second_hat) + adam_eps) + decay * param)
    return (new_param, jnp.stack([first, second]))


def adam_store(param, grad, moments, decay, new_param, new_moments):
    first = beta_first * moments[0] + (1.0 - beta_first) * grad
    second = beta_second * moments[1] + (1.0 - beta_second) * grad * grad
    first_hat = first * (1.0 / (1.0 - beta_first**step_count))
    second_hat = second * (1.0 / (1.0 - beta_second**step_count))
    step = first_hat / (jnp.sqrt(second_hat) + adam_eps) + decay * param
    new_param[...] = param - learn_rate * step
    new_moments[0][...] = first
    new_moments[1][...] = second


def adam_kernel(*refs):
    tot0, tot1, tot2, norm_ref, bias_ref, out_from, gin_from = refs[:7]
    params, moments = refs[7:11], refs[11:15]
    out_to, gin_to = refs[15:17]
    grads, new_params, new_moments = refs[17:21], refs[21:25], refs[25:29]
    held = (refs[29:32], refs[32:35])
    fresh = (refs[35:37], refs[37:39])
    pass_ref, pass_sem, in_sem, out_sem = refs[39:]
    width = params[0].shape[2]

    def place_of(index):
        if index == 3 or index >= 8:
            return 1, 0 if index == 3 else index - 7
        return 0, index if index < 3 else index - 1

    loads = [
        [
            pltpu.make_async_copy(params[group], held[group][0], in_sem.at[group, 0]),
            pltpu.make_async_copy(moments[group], held[group][1], in_sem.at[group, 1]),
        ]
        for group in range(2)
    ]
    for group in (1, 0):
        for copy in loads[group]:
            copy.start()
    passing = [
        pltpu.make_async_copy(source, pass_ref.at[spot], pass_sem.at[0, spot])
        for spot, source in enumerate((out_from, gin_from))
    ]
    for copy in passing:
        copy.start()
    stores = []
    for turn, (group, spots, indices) in enumerate(
        ((1, (1, 5), range(8, 12)), (0, (3, 7), range(4, 8)), (1, (0, 1), (3,)), (0, (0, 3), range(3)))
    ):
        if turn < 2:
            for copy in loads[group]:
                copy.wait()
        for index in indices:
            spot = place_of(index)[1]
            place = index % 4
            grad = (tot0, tot1, tot2)[index // 4][:, place * width : (place + 1) * width]
            if group:
                grad = grad.T
            held[group][2][spot] = grad
            adam_store(
                held[group][0][spot],
                grad,
                (held[group][1][0, spot], held[group][1][1, spot]),
                weight_decay,
                fresh[group][0].at[spot],
                (fresh[group][1].at[0, spot], fresh[group][1].at[1, spot]),
            )
        part = pl.ds(spots[0], spots[1] - spots[0])
        results = (
            (held[group][2].at[part], grads[group].at[part]),
            (fresh[group][0].at[part], new_params[group].at[part]),
            (fresh[group][1].at[:, part], new_moments[group].at[:, part]),
        )
        for place, (source, target) in enumerate(results):
            stores.append(pltpu.make_async_copy(source, target, out_sem.at[turn, place]))
            stores[-1].start()
        if turn == 0:
            for spot, target in enumerate((out_to, gin_to)):
                passing[spot].wait()
                stores.append(pltpu.make_async_copy(pass_ref.at[spot], target, pass_sem.at[1, spot]))
                stores[-1].start()
    norm_grad = jnp.concatenate([norm_ref[0, :6], norm_ref[1, :6]], 1)
    for group, grad in ((2, bias_ref[:6, :width]), (3, norm_grad)):
        grads[group][...] = grad
        adam_store(
            params[group][...],
            grad,
            (moments[group][:, 0, :], moments[group][:, 1, :]),
            0.0,
            new_params[group],
            (new_moments[group].at[:, 0, :], new_moments[group].at[:, 1, :]),
        )
    for copy in stores:
        copy.wait()


def update_here(rows, totals, params, moments):
    moments = moments[:2] + tuple(m.swapaxes(0, 1) for m in moments[2:])
    inside = pl.BlockSpec(memory_space=pltpu.VMEM)
    anywhere = pl.BlockSpec(memory_space=pl.ANY)
    kinds = [anywhere, anywhere, inside, inside]
    shapes = [jax.ShapeDtypeStruct(a.shape, jnp.float32) for a in params + params + moments]
    first, second, first_pair, second_pair = params[:2] + moments[:2]
    held = (first, first_pair, first, second, second_pair, second)
    fresh = (first, first_pair, second, second_pair)
    blocks = [pltpu.VMEM(a.shape, jnp.float32) for a in held + fresh]
    dma = pltpu.SemaphoreType.DMA
    results = pl.pallas_call(
        adam_kernel,
        out_shape=tuple(jax.ShapeDtypeStruct(a.shape, a.dtype) for a in rows) + tuple(shapes),
        in_specs=[inside] * len(totals) + [anywhere] * 2 + kinds * 2,
        out_specs=tuple([anywhere] * 2 + kinds * 3),
        scratch_shapes=blocks + [pltpu.VMEM((2,) + rows[0].shape, rows[0].dtype), dma((2, 2)), dma((2, 2)), dma((4, 3))],
        name="adam",
    )(*totals, *rows, *params, *moments)
    return results[:-2] + tuple(m.swapaxes(0, 1) for m in results[-2:])


def update_plain(share, rest, small, params, moments):
    group_width, width = params[0].shape[2], params[3].shape[1]
    total = jnp.concatenate([share, rest], 1)
    blocks = [total[:, k * group_width : (k + 1) * group_width] for k in range(12)]
    grads = (
        jnp.stack(blocks[:3] + blocks[4:8]),
        jnp.stack([blocks[3]] + blocks[8:]).swapaxes(1, 2),
        small[:6, width : width + group_width],
        small[:6, :width],
    )
    decays = (weight_decay, weight_decay, 0.0, 0.0)
    news = [adam_update(*group) for group in zip(params, grads, moments, decays)]
    return grads + tuple(n[0] for n in news) + tuple(n[1] for n in news)


def plain_layer(
    tokens,
    cotangent,
    lengths,
    in_weight,
    out_weight,
    in_bias,
    norm_vec,
    in_moments,
    out_moments,
    bias_moments,
    norm_moments,
):
    seq_count, seq_len, width = tokens.shape
    row_count = seq_count * seq_len
    in_low = in_weight.astype(jnp.bfloat16)
    out_low = out_weight.astype(jnp.bfloat16).swapaxes(1, 2)
    share = jnp.concatenate(list(in_low[:3]) + [out_low[0]], 1)
    rest = jnp.concatenate(list(in_low[3:]) + list(out_low[1:]), 1)
    first_full = lax.all_gather(share, "dp", axis=0, tiled=True)
    second_full = lax.all_gather(rest, "dp", axis=0, tiled=True)
    group_width = in_weight.shape[2]
    heads_here = group_width // HDIM
    w_qkv = first_full[:, : 3 * group_width]
    w_proj = first_full[:, 3 * group_width :]
    bias_up = in_bias[2:6].reshape(1, 4 * group_width)

    def split_heads(flat_rows):
        return flat_rows.reshape(seq_count, seq_len, heads_here, HDIM)

    flat_tokens = tokens.reshape(row_count, width)
    qkv = matmul(flat_tokens, w_qkv)
    query = (qkv[:, :group_width] + in_bias[0]).astype(jnp.bfloat16)
    keys_low = qkv[:, group_width : 2 * group_width].astype(jnp.bfloat16)
    values_low = (qkv[:, 2 * group_width :] + in_bias[1]).astype(jnp.bfloat16)
    mixed_heads, log_total = lax.map(
        attend_forward,
        (split_heads(query), split_heads(keys_low), split_heads(values_low), lengths),
    )
    mixed_flat = mixed_heads.reshape(row_count, group_width)
    attn_part = times_transposed(mixed_flat, w_proj).astype(jnp.bfloat16)
    attn_out = lax.psum(attn_part, "tensor")
    w_up = second_full[:, : 4 * group_width]
    w_down = second_full[:, 4 * group_width :]
    hidden, normed_one, inverse_one = layer_norm(
        flat_tokens.astype(jnp.float32) + attn_out.astype(jnp.float32) + norm_vec[0], norm_vec[1], norm_vec[2]
    )
    hidden_low = hidden.astype(jnp.bfloat16)
    pre_act = matmul(hidden_low, w_up) + bias_up
    act_low = gelu_value(pre_act).astype(jnp.bfloat16)
    ffn_part = times_transposed(act_low, w_down).astype(jnp.bfloat16)
    ffn_out = lax.psum(ffn_part, "tensor").astype(jnp.float32)
    out_rows, normed_two, inverse_two = layer_norm(
        hidden + ffn_out + norm_vec[3], norm_vec[4], norm_vec[5]
    )
    positions = lax.broadcasted_iota(jnp.int32, (seq_count, seq_len), 1)
    live_rows = (positions < lengths[:, None]).astype(jnp.float32).reshape(row_count, 1)
    grad_out = cotangent.reshape(row_count, width).astype(jnp.float32) * live_rows
    grad_two = norm_back(grad_out, normed_two, inverse_two, norm_vec[4])
    grad_two_low = grad_two.astype(jnp.bfloat16)
    grad_down = inner_rows(grad_two_low, act_low).astype(jnp.bfloat16)
    grad_act = matmul(grad_two_low, w_down)
    grad_pre = grad_act * gelu_slope(pre_act)
    grad_pre_low = grad_pre.astype(jnp.bfloat16)
    grad_up = inner_rows(hidden_low, grad_pre_low).astype(jnp.bfloat16)
    rest_grads = jnp.concatenate([grad_up, grad_down], 1)
    back_part = times_transposed(grad_pre_low, w_up).astype(jnp.bfloat16)
    back_sum = lax.psum(back_part, "tensor")
    grad_hidden = grad_two + back_sum.astype(jnp.float32)
    grad_one = norm_back(grad_hidden, normed_one, inverse_one, norm_vec[1])
    grad_one_low = grad_one.astype(jnp.bfloat16)
    grad_proj = inner_rows(grad_one_low, mixed_flat).astype(jnp.bfloat16)
    grad_mixed = matmul(grad_one_low, w_proj).astype(jnp.bfloat16)
    grad_query, grad_keys, grad_values = lax.map(
        attend_backward,
        (
            split_heads(query),
            split_heads(keys_low),
            split_heads(values_low),
            split_heads(grad_mixed),
            log_total,
            lengths,
        ),
    )
    grad_query = grad_query.reshape(row_count, group_width)
    grad_keys = grad_keys.reshape(row_count, group_width)
    grad_values = grad_values.reshape(row_count, group_width)
    qkv_grad_low = jnp.concatenate([grad_query, grad_keys, grad_values], 1).astype(jnp.bfloat16)
    input_part = times_transposed(qkv_grad_low, w_qkv).astype(jnp.bfloat16)
    grad_qkv = inner_rows(flat_tokens, qkv_grad_low).astype(jnp.bfloat16)
    first_grads = jnp.concatenate([grad_qkv, grad_proj], 1)
    bias_rows = jnp.concatenate(
        [jnp.sum(grad_query, 0), jnp.sum(grad_values, 0), jnp.sum(grad_pre, 0)]
    ).reshape(6, group_width)
    norm_rows = jnp.stack(
        [
            jnp.sum(grad_one, 0),
            jnp.sum(grad_hidden * normed_one, 0),
            jnp.sum(grad_hidden, 0),
            jnp.sum(grad_two, 0),
            jnp.sum(grad_out * normed_two, 0),
            jnp.sum(grad_out, 0),
        ]
    )
    small = jnp.pad(jnp.concatenate([norm_rows, bias_rows], 1), ((0, 2), (0, 64)))
    share_total = scatter_plain(first_grads)
    rest_total = scatter_plain(rest_grads)
    input_sum = lax.psum(input_part, "tensor")
    small_total = lax.psum(small, "dp")
    grad_input = grad_one + input_sum.astype(jnp.float32)
    params = (in_weight, out_weight, in_bias, norm_vec)
    moments = (in_moments, out_moments, bias_moments, norm_moments)
    updates = update_plain(share_total, rest_total, small_total, params, moments)
    output = out_rows.astype(jnp.bfloat16).reshape(seq_count, seq_len, width)
    grad_tokens = grad_input.astype(jnp.bfloat16).reshape(seq_count, seq_len, width)
    return (
        output,
        grad_tokens,
    ) + tuple(updates)


def local(*operands):
    tokens, cotangent, lengths, in_weight, out_weight, in_bias, norm_vec = operands[:7]
    ring = lax.axis_size("dp") == RING and lax.axis_size("tensor") == 4
    if not ring or tokens.shape[0] != 1:
        return plain_layer(*operands)
    out, grad_tokens, *totals = run_layer(
        tokens[0], cotangent[0], lengths, in_weight, out_weight, in_bias, norm_vec
    )
    results = update_here((out, grad_tokens), tuple(totals), operands[3:7], operands[7:])
    return (results[0][None], results[1][None]) + tuple(results[2:])


def solution(mesh):
    in_specs = (
        P("dp", None, None),
        P("dp", None, None),
        P("dp"),
        P(None, "dp", "tensor"),
        P(None, "tensor", "dp"),
        P(None, "tensor"),
        P(),
        P(None, None, "dp", "tensor"),
        P(None, None, "tensor", "dp"),
        P(None, None, "tensor"),
        P(),
    )
    out_specs = (
        P("dp", None, None),
        P("dp", None, None),
        P(None, "dp", "tensor"),
        P(None, "tensor", "dp"),
        P(None, "tensor"),
        P(),
        P(None, "dp", "tensor"),
        P(None, "tensor", "dp"),
        P(None, "tensor"),
        P(),
        P(None, None, "dp", "tensor"),
        P(None, None, "tensor", "dp"),
        P(None, None, "tensor"),
        P(),
    )
    return jax.shard_map(local, mesh=mesh, in_specs=in_specs, out_specs=out_specs, check_vma=False)
```
